32 devices in a mesh: groups: 2 (over x), sky: 16 (over z, y, core).
Axes of the slice: x: 2, y: 2, z: 4, core: 2. Of those that a mesh axis runs over, the one named last changes fastest.
Arguments:
- image: bfloat16 [32, 512, 128], P(('groups', 'sky')), parts along dimension 0, may hold values from -6 to 6
- row_taps: bfloat16 [40, 31], replicated, may hold values from -1 to 1
- col_taps: bfloat16 [40, 31], replicated, may hold values from -1 to 1
- mix_coeff: float32 [32, 3, 40], P(('groups', 'sky')), parts along dimension 0, may hold values from -1 to 1
- shift_frac: float32 [32, 2], P(('groups', 'sky')), parts along dimension 0, may hold values from 0.05 to 0.95
- ccd_visit: int32 [32], P(('groups', 'sky')), parts along dimension 0, may hold values from 0 to 3
- visit_weight: bfloat16 [8], P('groups'), parts along dimension 0, may hold values from 0.25 to 4
- tile_block: int32 [2048], P(('groups', 'sky')), parts along dimension 0, may hold values from 0 to 255, as said below
- tile_offset: int32 [2048], P(('groups', 'sky')), parts along dimension 0, may hold values from 0 to 7
Outputs:
- coadd: float32 [4096, 128], P(('groups', 'sky')), parts along dimension 0
- weight_map: float32 [4096], P(('groups', 'sky')), parts along dimension 0
The draws below stay inside these ranges and needn't reach their ends.
There are 2 independent parts, one for each index of `groups`. The reference program is written for one: setup_inputs(seed, part) draws one part's arguments, and reference() takes and returns one part's arrays. A program takes and returns all parts, laid end to end along the dimension named above; an argument that names none is the same for every part. Nothing has to cross between parts.
Inputs may be any that keep to these rules, and one draw needn't show every extreme that they name: `tile_block`: the owner of sky block b is device b // 16 of the sky axis. The 64 tiles of one window go to exactly 16 distinct owners, 4 tiles to each; at least four owners receive 4 tiles from every window.
All inputs are finite; a program needn't handle non-finite values.
Results may differ from the reference program's by a relative error of at most 0.0041.
Values may be sent and summed in bfloat16 or wider, within the bound.
A program may use at most 64 MiB of HBM per device.

```python
import math
import jax
import jax.numpy as jnp
from jax import lax

K = 40
TAPS = 31
VISITS = 4
TILE_R = 8
WC = 128
WR = 512
TILES_DEV = 64
CAP = 4
BLK_DEV = 16
SKY_HOLDERS = 16
CCDS = 16
TILES = 1024
SKY_ROWS = 2048


def draw_tile_block(key, part):
    keys = jax.random.split(jax.random.fold_in(key, 17), 5)
    dest_count = TILES_DEV // CAP
    demand_tally = jax.random.randint(keys[0], (SKY_HOLDERS,), 0, 2 ** 20)
    central_ranking = jax.random.permutation(keys[1], SKY_HOLDERS)
    central_reward = jnp.where(central_ranking < 4, 2 ** 22, 0)
    random_perturbation = jax.random.randint(keys[2], (SKY_HOLDERS, SKY_HOLDERS), 0, 2 ** 20)
    priority_values = (demand_tally[None, :] + central_reward[None, :] + random_perturbation) * SKY_HOLDERS + jnp.arange(SKY_HOLDERS)[None, :]
    priority_values = priority_values.astype(jnp.int32)
    unused_values, chosen = lax.top_k(priority_values, dest_count)
    shuffles = jax.vmap(lambda derived_random_key: jax.random.permutation(derived_random_key, TILES_DEV))(jax.random.split(keys[3], SKY_HOLDERS))
    owners = jnp.take_along_axis(chosen, shuffles // CAP, axis=1)
    local_block = jax.random.randint(keys[4], (SKY_HOLDERS, TILES_DEV), 0, BLK_DEV)
    return (owners * BLK_DEV + local_block).reshape(-1).astype(jnp.int32)


def plant(array, key, low, largest):
    extent = array.shape
    spot = [jax.random.randint(jax.random.fold_in(key, axis), (), 0, extent[axis]) for axis in range(len(extent))]
    array = array.at[tuple(spot)].set(low)
    longest = extent.index(max(extent))
    spot[longest] = (spot[longest] + 1) % extent[longest]
    return array.at[tuple(spot)].set(largest)


def steps_of(rng, dims, shards, smallest, largest):
    def one(position, blocks):
        steps = jax.random.uniform(jax.random.fold_in(jax.random.fold_in(rng, 6), position), (blocks,), jnp.float32, smallest / len(shards), largest / len(shards))
        return jnp.repeat(jnp.exp(steps), dims[position] // blocks).reshape((-1,) + (1,) * (len(dims) - position - 1))

    level = one(*shards[0])
    for cut in shards[1:]:
        level = level * one(*cut)
    return level


def bell_draw(rng, dims, deviation, reach, shards=(), held_as=jnp.bfloat16):
    values = jax.random.normal(rng, dims, jnp.float32) * deviation
    if len(shards) > 0:
        values = steps_of(rng, dims, shards, -0.22, 0.18) * values
    return jnp.clip(values, min=-reach, max=reach).astype(held_as)


def setup_inputs(seed: int = 0, part: int = 0) -> dict:
    streams_of = jax.random.split(jax.random.key(seed), 10)
    part_splits = jax.random.split(jax.random.fold_in(streams_of[9], part), 10)
    image = bell_draw(part_splits[0], (CCDS, WR, WC), 1.0, 6.0, ((0, 16),))
    row_taps = bell_draw(streams_of[1], (K, TAPS), TAPS ** -0.5, 1.0)
    col_taps = bell_draw(streams_of[2], (K, TAPS), TAPS ** -0.5, 1.0)
    mix_coeff = bell_draw(part_splits[3], (CCDS, 3, K), K ** -0.5, 1.0, ((0, 16),), jnp.float32)
    shift_frac = jnp.clip(0.05 + 0.9 * jax.random.uniform(part_splits[4], (CCDS, 2), jnp.float32) ** steps_of(part_splits[4], (CCDS, 2), ((0, 16),), -0.2, 0.2), 0.05, 0.95)
    ccd_visit = plant(jax.random.randint(part_splits[5], (CCDS,), 0, VISITS), jax.random.fold_in(part_splits[5], 1), 0, VISITS - 1).astype(jnp.int32)
    visit_weight = jnp.clip(jnp.exp(jax.random.uniform(part_splits[6], (VISITS,), jnp.float32, math.log(0.25), math.log(4.0))), 0.25, 4.0).astype(jnp.bfloat16)
    tile_block = draw_tile_block(jax.random.fold_in(jax.random.fold_in(streams_of[9], part), 71), part)
    tile_offset = plant(jax.random.randint(part_splits[8], (TILES,), 0, TILE_R), jax.random.fold_in(part_splits[8], 1), 0, TILE_R - 1).astype(jnp.int32)
    return {"image": image, "row_taps": row_taps, "col_taps": col_taps, "mix_coeff": mix_coeff, "shift_frac": shift_frac, "ccd_visit": ccd_visit, "visit_weight": visit_weight, "tile_block": tile_block, "tile_offset": tile_offset}


def lanczos_taps(fraction):
    positions = jnp.arange(-2, 4).astype(jnp.float32)
    offsets = positions[None, :] - fraction[:, None]
    angles = jnp.pi * offsets
    kernel = jnp.sin(angles) / angles * (jnp.sin(angles / 3.0) / (angles / 3.0))
    return kernel / jnp.sum(kernel, axis=1, keepdims=True)


def match_window(window, row_taps, col_taps, coefficients):
    half_taps = (TAPS - 1) // 2
    pixels = window.astype(jnp.float32)[None, None]
    kernel_row = row_taps.astype(jnp.float32)[:, None, None, :]
    smoothed = lax.conv_general_dilated(pixels, kernel_row, (1, 1), ((0, 0), (half_taps, half_taps)), dimension_numbers=("NCHW", "OIHW", "NCHW"), precision=lax.Precision.HIGHEST)
    smoothed = lax.optimization_barrier(smoothed.astype(jnp.bfloat16)).astype(jnp.float32)
    kernel_col = col_taps.astype(jnp.float32)[:, None, :, None]
    vertical = lax.conv_general_dilated(smoothed, kernel_col, (1, 1), ((half_taps, half_taps), (0, 0)), dimension_numbers=("NCHW", "OIHW", "NCHW"), feature_group_count=K, precision=lax.Precision.HIGHEST)[0]
    column_pos = (2.0 * jnp.arange(WC).astype(jnp.float32) + 1.0) / WC - 1.0
    row_pos = (2.0 * jnp.arange(WR).astype(jnp.float32) + 1.0) / WR - 1.0
    weights = coefficients[0][:, None, None] + coefficients[1][:, None, None] * column_pos[None, None, :] + coefficients[2][:, None, None] * row_pos[None, :, None]
    return jnp.sum(weights * vertical, axis=0)


def warp_window(matched, fraction):
    taps_across = lanczos_taps(fraction[1:2])[0]
    taps_down = lanczos_taps(fraction[0:1])[0]
    padded = jnp.pad(matched, ((0, 0), (2, 3)))
    spread = taps_across[0] * padded[:, 0:WC]
    for offset_index in range(1, 6):
        spread = spread + taps_across[offset_index] * padded[:, offset_index:offset_index + WC]
    padded = jnp.pad(spread, ((2, 3), (0, 0)))
    warped = taps_down[0] * padded[0:WR]
    for offset_index in range(1, 6):
        warped = warped + taps_down[offset_index] * padded[offset_index:offset_index + WR]
    return warped.astype(jnp.bfloat16)


def reference(image, row_taps, col_taps, mix_coeff, shift_frac, ccd_visit, visit_weight, tile_block, tile_offset):
    def one_window(packed):
        window, coefficients, fraction = packed
        return warp_window(match_window(window, row_taps, col_taps, coefficients), fraction)

    warped = lax.map(one_window, (image, mix_coeff, shift_frac))
    visit_match = ccd_visit[:, None] == jnp.arange(VISITS)[None, :]
    ccd_weight = jnp.sum(jnp.where(visit_match, visit_weight.astype(jnp.float32)[None, :], 0.0), axis=1)
    tile_weight = jnp.repeat(ccd_weight, TILES_DEV)
    tile_pixels = warped.reshape(CCDS * TILES_DEV, TILE_R, WC).astype(jnp.float32)
    weighted = tile_pixels * tile_weight[:, None, None]
    row_index = (tile_block[:, None] * TILE_R + tile_offset[:, None] + jnp.arange(TILE_R)[None, :]).astype(jnp.int32)
    sky_sum = jax.ops.segment_sum(weighted.reshape(-1, WC), row_index.reshape(-1), num_segments=SKY_ROWS + TILE_R)[:SKY_ROWS]
    row_weight = jnp.broadcast_to(tile_weight[:, None], (CCDS * TILES_DEV, TILE_R))
    weight_map = jax.ops.segment_sum(row_weight.reshape(-1), row_index.reshape(-1), num_segments=SKY_ROWS + TILE_R)[:SKY_ROWS]
    coadd = sky_sum / jnp.maximum(weight_map, 1.0)[:, None]
    return coadd, weight_map
```

```python
import functools

import jax
import jax.numpy as jnp
from jax import lax
from jax.experimental import pallas as pl
from jax.experimental.pallas import tpu as pltpu
from jax.sharding import PartitionSpec as P

TILE_R = 8
BLK_DEV = 16
LANES = 128
F32 = jnp.float32
BF16 = jnp.bfloat16


def iota(shape, axis):
    return lax.broadcasted_iota(jnp.int32, shape, axis)


def dot(lhs, rhs):
    return jnp.dot(lhs, rhs, preferred_element_type=F32)


def onehot(mask):
    return jnp.where(mask, 1.0, 0.0).astype(BF16)


def lanczos(fraction):
    lane = iota((1, LANES), 1)
    offsets = (lane - 2).astype(F32) - fraction
    offsets = jnp.where(lane < 6, offsets, 0.5)
    angles = jnp.pi * offsets
    thirds = angles / 3.0
    kernel = jnp.sin(angles) / angles * (jnp.sin(thirds) / thirds)
    kernel = jnp.where(lane < 6, kernel, 0.0)
    return kernel / jnp.sum(kernel, axis=1, keepdims=True)


def kernel(
    sky,
    *refs,
):
    sources = refs[0:9]
    result_ref = refs[9]
    (
        image_ref,
        row_taps_ref,
        col_taps_ref,
        mix_ref,
        shift_ref,
        visit_ref,
        visit_weight_ref,
        block_ref,
        offset_ref,
    ) = held = refs[10:19]
    (
        xpad,
        pairs,
        edges,
        quads,
        body,
        rim,
        pick,
        taps2d,
        acc,
        spread_pad,
        data_send,
        data_recv,
        load_sem,
        data_ssem,
        data_rsem,
    ) = refs[19:]
    loads = [
        pltpu.make_async_copy(source, target, load_sem.at[number])
        for number, (source, target) in enumerate(zip(sources, held))
    ]
    for number in (1, 2, 3, 0, 7, 8, 5, 6, 4):
        loads[number].start()
    me = lax.axis_index("sky")
    win_rows, win_cols = image_ref.shape
    tap_count, basis = row_taps_ref.shape
    half = tap_count // 2
    tiles = block_ref.shape[1]
    cap = max(2, tiles // sky)
    span = cap * TILE_R
    owned_rows = BLK_DEV * TILE_R
    blk_shift = BLK_DEV.bit_length() - 1

    barrier = pltpu.get_barrier_semaphore()

    def greet(step, carry):
        pl.semaphore_signal(
            barrier,
            inc=1,
            device_id={"sky": lax.rem(me + step, sky)},
            device_id_type=pl.DeviceIdType.MESH,
        )
        return carry

    lax.fori_loop(1, sky, greet, 0)

    xpad[0:16, :] = jnp.zeros((16, win_cols), F32)
    xpad[win_rows + 16 :, :] = jnp.zeros((xpad.shape[0] - win_rows - 16, win_cols), F32)
    for number in (1, 2, 3):
        loads[number].wait()

    def message(send, recv, ssem, rsem, turn):
        to = turn - 1 + lax.div(turn - 1 - me + sky, jnp.int32(sky))
        return pltpu.make_async_remote_copy(
            src_ref=send.at[to],
            dst_ref=recv.at[me],
            send_sem=ssem,
            recv_sem=rsem,
            device_id={"sky": to},
            device_id_type=pl.DeviceIdType.MESH,
        )

    def wait_all(send, recv, ssem, rsem):
        copy = pltpu.make_async_remote_copy(
            src_ref=send.at[pl.ds(0, sky - 1)],
            dst_ref=recv.at[pl.ds(0, sky - 1)],
            send_sem=ssem,
            recv_sem=rsem,
            device_id={"sky": lax.rem(me + 1, sky)},
            device_id_type=pl.DeviceIdType.MESH,
        )
        copy.wait_send()
        copy.wait_recv()

    tap = iota((tap_count, 2 * LANES), 0)
    spot = iota((tap_count, 2 * LANES), 1)
    place = jnp.where(spot < LANES, 0, LANES // 2)
    flip = onehot(
        lax.rem(spot, jnp.int32(LANES)) == lax.rem(half + place - tap + LANES, jnp.int32(LANES))
    )
    flipped = lax.dot_general(
        row_taps_ref[...], flip, (((0,), (0,)), ((), ())), preferred_element_type=F32
    ).astype(BF16)
    near, far = flipped[:, 0:LANES], flipped[:, LANES:]

    def mixed(term, taps):
        value = col_taps_ref[...].astype(F32) * mix_ref[term]
        high = value.astype(BF16)
        low = (value - high.astype(F32)).astype(BF16)
        return dot(high, taps) + dot(low, taps)

    taps2d[0, 0:tap_count, :] = mixed(0, near) + mixed(2, far)
    taps2d[1, 0:tap_count, :] = mixed(1, near)

    side = win_cols // 2
    edge = 16
    pair_rows = win_rows // 2
    shifts = (tap_count + 1) // 2
    eight = (TILE_R, LANES)
    group = (edge, LANES)
    lane_of = iota(eight, 1)
    signed = lax.rem(lane_of + side, jnp.int32(LANES)) - side
    column_pos = (2.0 * signed.astype(F32) + 1.0) / win_cols - 1.0
    in_side = lax.rem(iota(group, 1), jnp.int32(side))
    inside = {
        first: onehot(jnp.abs(iota(group, 0) + first - in_side) <= half)
        for first in range(-edge, side + edge, edge)
        if first < half or first + edge + half > side
    }

    def toeplitz(tap):
        fixed, slope = (
            pltpu.roll(
                jnp.broadcast_to(taps2d[term, tap : tap + 1, :], eight),
                0,
                1,
                stride=1,
                stride_axis=0,
            )
            for term in range(2)
        )
        fixed = fixed + column_pos * slope
        lower = pltpu.roll(fixed + (2.0 * TILE_R / win_cols) * slope, TILE_R, 1)
        value = jnp.concatenate([fixed, lower], axis=0)
        step = jnp.concatenate([slope, pltpu.roll(slope, TILE_R, 1)], axis=0)
        step = (2.0 * edge / win_cols) * step
        for column in range(0, win_cols, edge):
            rounded = value.astype(BF16)
            for part in range(2):
                first = column - side * part
                if -edge * part <= first < side + edge * (1 - part):
                    rows = pltpu.roll(rounded, first % LANES, 1) if first else rounded
                    if first in inside:
                        rows = rows * inside[first]
                    if 0 <= first < side:
                        row = (tap + 1) * side + first
                        body[part, row : row + edge, :] = rows
                    else:
                        row = (tap + 1) * edge
                        rim[part, row : row + edge, :] = rows
            value = value + step

    for part in range(2):
        for row in (0, (tap_count + 1) * side):
            body[part, row : row + side, :] = jnp.zeros((side, LANES), BF16)
        for row in (0, (tap_count + 1) * edge):
            rim[part, row : row + edge, :] = jnp.zeros(group, BF16)

    for tap in range(8):
        toeplitz(tap)
    for number in (4, 5, 6, 7, 8, 0):
        loads[number].wait()
    xpad[pl.ds(16, win_rows), :] = image_ref[...].astype(F32)
    held_rows = pairs.shape[1]
    lane_of = iota((held_rows, LANES), 1)
    low = onehot(lane_of < side)
    high = onehot(lane_of >= side)
    odd = xpad[pl.ds(1, held_rows, stride=2), :].astype(BF16)
    even = xpad[pl.ds(2, held_rows, stride=2), :].astype(BF16)
    west = odd * low + pltpu.roll(even, side, 1) * high
    east = pltpu.roll(odd, side, 1) * low + even * high
    pairs[0] = west.astype(F32)
    pairs[1] = east.astype(F32)

    for tap in range(8, tap_count):
        toeplitz(tap)

    block = block_ref[...]
    owner_i = lax.shift_right_logical(block, blk_shift)
    start_row = ((block - owner_i * BLK_DEV) * TILE_R + offset_ref[...]).astype(F32)
    owner_row = owner_i.astype(F32)
    eye = iota((tiles, tiles), 0) == iota((tiles, tiles), 1)
    column = lambda row: jnp.sum(
        jnp.where(eye, jnp.broadcast_to(row, (tiles, tiles)), 0.0), axis=1, keepdims=True
    )
    owner_col = column(owner_row)
    start_col = column(start_row)
    same = owner_col == owner_row
    below = iota((tiles, tiles), 0) < iota((tiles, tiles), 1)
    above = iota((tiles, tiles), 1) < iota((tiles, tiles), 0)
    rank_row = jnp.sum(jnp.where(same & below, 1.0, 0.0), axis=0, keepdims=True)
    rank_col = jnp.sum(jnp.where(same & above, 1.0, 0.0), axis=1, keepdims=True)
    visits = visit_weight_ref.shape[1]
    own_weight = jnp.sum(
        jnp.where(
            iota((1, visits), 1) == visit_ref[...], visit_weight_ref[...].astype(F32), 0.0
        ),
        axis=1,
        keepdims=True,
    )

    per_group = LANES // span
    spill_group = min(LANES // TILE_R, sky)
    sub = iota((sky * TILE_R, tiles), 0)
    owner_of = lax.shift_right_logical(sub, 3).astype(F32)
    lane = iota((tiles, LANES), 1)
    mine = lax.div(lane, jnp.int32(span)) == lax.rem(me, per_group)
    local = lax.rem(lane, jnp.int32(span))
    parity = lax.div(local, jnp.int32(span // 2))
    local = lax.rem(local, jnp.int32(span // 2))
    slot_rank = lax.div(local, jnp.int32(TILE_R // 2)).astype(F32)
    in_eight = (2 * lax.rem(local, jnp.int32(TILE_R // 2)) + parity).astype(F32)
    landing = jnp.where(mine & (slot_rank == rank_col), start_col + in_eight + 1.0, 0.0)
    in_eight = lax.rem(lane, jnp.int32(TILE_R)).astype(F32)
    targets = dot(onehot(owner_of == owner_row), landing.astype(BF16))
    mine = lax.div(lane, jnp.int32(TILE_R)) == lax.rem(me, spill_group)
    cover = onehot(mine & (start_col > in_eight + float(owned_rows - TILE_R)))
    covered = dot(onehot(owner_of - 1.0 == owner_row), cover)
    lane8 = iota((sky * TILE_R, LANES), 1)
    sub8 = lax.rem(iota((sky * TILE_R, LANES), 0), jnp.int32(TILE_R))
    weight8 = jnp.broadcast_to(own_weight, (sky * TILE_R, LANES))
    tile_lanes = lax.div(lane8, jnp.int32(span)) == lax.rem(me, per_group)
    spill_lanes = lax.div(lane8, jnp.int32(TILE_R)) == lax.rem(me, spill_group)
    header = jnp.where((sub8 == 1) & tile_lanes, weight8, 0.0)
    header = jnp.where((sub8 == 2) & spill_lanes, weight8, header)
    header = jnp.where(sub8 == 3, covered, header)
    header = jnp.where(sub8 == 0, targets, header)
    data_send[:, span + TILE_R :, :] = header.reshape(sky, TILE_R, LANES).astype(BF16)

    wide = tiles * TILE_R // 2
    widen = onehot(
        iota((tiles, wide), 0) == lax.shift_right_logical(iota((tiles, wide), 1), 2)
    )
    in_tile = (2 * lax.rem(iota((1, wide), 1), jnp.int32(TILE_R // 2))).astype(F32)
    spread8 = lambda row: dot(jnp.broadcast_to(row, (8, tiles)).astype(BF16), widen)[0:1, :]
    owner_wide = spread8(owner_row)
    slot_lane = spread8(owner_row * cap + rank_row) * (TILE_R // 2) + in_tile / 2.0
    sent = sky * span // 2
    past = spread8(start_row) + in_tile - float(owned_rows)
    pick[0:sent, :] = onehot(iota((sent, wide), 0).astype(F32) == slot_lane)
    spills = sky * TILE_R
    for parity in range(2):
        moved = past + float(parity)
        spill_lane = jnp.where(moved >= 0.0, (owner_wide + 1.0) * TILE_R + moved, -1.0)
        pick[sent + parity * spills : sent + (parity + 1) * spills, :] = onehot(
            iota((spills, wide), 0).astype(F32) == spill_lane
        )

    low = onehot(lane_of < edge)
    high = onehot((lane_of >= edge) & (lane_of < 2 * edge))
    quad_rows = quads.shape[1]
    quarter = lax.div(iota((quad_rows, LANES), 1), jnp.int32(2 * edge))
    for part in range(2):
        if part:
            strip = pltpu.roll(west, edge + side, 1) * low + pltpu.roll(west, 2 * edge, 1) * high
        else:
            strip = east * low + pltpu.roll(east, edge + side, 1) * high
        strip = strip + pltpu.roll(strip, 2 * edge, 1)
        strip = strip + pltpu.roll(strip, 4 * edge, 1)
        edges[part] = strip.astype(F32)
        value = edges[part, 0:quad_rows, :]
        for later in range(1, 4):
            value = jnp.where(quarter == later, edges[part, pl.ds(later, quad_rows), :], value)
        quads[part] = value

    def product(part, first, last):
        left = [pairs[part, pl.ds(shift, pair_rows), :].astype(BF16) for shift in range(first, last)]
        first, last = 2 * side * first, 2 * side * last
        weights = [body[part, first + side : last + side, :], body[part, first:last, :]]
        return dot(jnp.concatenate(left, axis=1), jnp.concatenate(weights, axis=1))

    def border(part):
        left = [
            quads[part, pl.ds(first, pair_rows), :].astype(BF16) for first in range(0, shifts, 4)
        ]
        last = (tap_count + 1) * edge
        weights = [rim[part, edge : last + edge, :], rim[part, 0:last, :]]
        return dot(jnp.concatenate(left, axis=1), jnp.concatenate(weights, axis=1))

    for part in range(2):
        acc[part] = product(part, 0, shifts) + border(part)

    across = lanczos(shift_ref[0:1, 1:2])
    down = lanczos(shift_ref[0:1, 0:1])
    chunk = min(64, pair_rows)
    for parity in range(2):
        spread_pad[parity, 0:8, :] = jnp.zeros((8, win_cols), F32)
        spread_pad[parity, pair_rows + 8 :, :] = jnp.zeros((8, win_cols), F32)
    down_taps = [
        jnp.broadcast_to(down[0:1, m + 2 : m + 3], (1, win_cols)) for m in range(-2, 4)
    ]
    square = (2 * LANES, LANES)
    pixel = lax.div(iota(square, 0), jnp.int32(LANES)) * side + lax.rem(
        iota(square, 0), jnp.int32(side)
    )
    warp = jnp.zeros(square, F32)
    for m in range(-2, 4):
        warp = jnp.where(pixel - iota(square, 1) == m, across[0:1, m + 2 : m + 3], warp)
    warp_high = warp.astype(BF16)
    warp_low = (warp - warp_high.astype(F32)).astype(BF16)
    warp_both = jnp.concatenate([warp_high, warp_low], axis=1)
    in_first = iota((chunk, LANES), 1) < side
    for first in range(0, pair_rows, chunk):
        here = slice(first, first + chunk)
        for parity in range(2):
            columns = slice(parity * LANES, (parity + 1) * LANES)
            row_pos = (2 * (iota((chunk, LANES), 0) + first) + parity).astype(F32)
            row_pos = (2.0 * row_pos + 1.0) / win_rows - 1.0
            factor = jnp.where(in_first, 1.0, row_pos)
            terms = jnp.concatenate(
                [acc[0, here, columns] * factor, acc[1, here, columns] * factor], axis=1
            )
            high = terms.astype(BF16)
            low = (terms - high.astype(F32)).astype(BF16)
            both = dot(high, warp_both)
            spread = both[:, 0:LANES] + both[:, LANES:] + dot(low, warp_high)
            spread_pad[parity, first + 8 : first + 8 + chunk, :] = spread
    warped = []
    for parity in range(2):
        rows = []
        for first in range(0, pair_rows, chunk):
            value = None
            for m in range(-2, 4):
                other = (parity + m) % 2
                down_by = (parity + m - other) // 2
                term = down_taps[m + 2] * spread_pad[other, pl.ds(first + 8 + down_by, chunk), :]
                value = term if value is None else value + term
            rows.append(value.astype(BF16))
        warped.append(jnp.concatenate(rows, axis=0))
    warped = jnp.concatenate(warped, axis=1)

    packed = dot(pick[...], warped)
    tile_rows = (sky, span // 2, win_cols)
    tile_rows = [packed[0:sent, columns].reshape(tile_rows) for columns in (slice(0, LANES), slice(LANES, 2 * LANES))]
    data_send[:, 0:span, :] = jnp.concatenate(tile_rows, axis=1).astype(BF16)
    spilled = packed[sent : sent + spills, 0:LANES] + packed[sent + spills :, LANES:]
    data_send[:, span : span + TILE_R, :] = spilled.reshape(sky, TILE_R, win_cols).astype(BF16)

    def start_data(step, carry):
        message(data_send, data_recv, data_ssem, data_rsem, step).start()
        return carry

    pl.semaphore_wait(barrier, sky - 1)
    lax.fori_loop(1, sky, start_data, 0)
    data_recv[pl.ds(me, 1)] = data_send[pl.ds(me, 1)]

    wait_all(data_send, data_recv, data_ssem, data_rsem)

    owned = (owned_rows, LANES)
    row_id = (iota(owned, 0) + 1).astype(F32)
    places = []
    total = jnp.zeros((owned_rows, win_cols), F32)
    ones = jnp.ones((LANES, win_cols), BF16)
    for group in range(sky // per_group):
        head = data_recv[group * per_group : (group + 1) * per_group, span + TILE_R :, :]
        head = jnp.sum(head.astype(F32), axis=0)
        place = jnp.where(head[0:1, :] == row_id, head[1:2, :], 0.0).astype(BF16)
        places.append(place)
        total = total + dot(place, ones)
    spill_places = []
    same_row = lax.rem(iota(owned, 1), jnp.int32(TILE_R)) == iota(owned, 0)
    here_row = lax.rem(iota(eight, 1), jnp.int32(TILE_R)) == iota(eight, 0)
    first_rows = jnp.zeros(eight, F32)
    for group in range(sky // spill_group):
        head = data_recv[group * spill_group : (group + 1) * spill_group, span + TILE_R :, :]
        head = jnp.sum(head.astype(F32), axis=0)
        spill_places.append(jnp.where(same_row, head[2:3, :], 0.0).astype(BF16))
        count = jnp.sum(jnp.where(here_row, head[2:3, :] * head[3:4, :], 0.0), axis=1, keepdims=True)
        first_rows = first_rows + jnp.broadcast_to(count, eight)
    total = total + jnp.concatenate(
        [first_rows, jnp.zeros((owned_rows - TILE_R, LANES), F32)], axis=0
    )
    diagonal = iota(owned, 0) == iota(owned, 1)
    result_ref[owned_rows:, :] = jnp.broadcast_to(
        jnp.sum(jnp.where(diagonal, total, 0.0), axis=0, keepdims=True), (8, LANES)
    )

    sums = jnp.zeros((owned_rows, win_cols), F32)
    for group, place in enumerate(places):
        part = data_recv[group * per_group : (group + 1) * per_group, 0:span, :]
        sums = sums + dot(place, part.reshape(LANES, win_cols))
    for group, place in enumerate(spill_places):
        part = data_recv[group * spill_group : (group + 1) * spill_group, span : span + TILE_R, :]
        part = part.astype(F32).reshape(spill_group * TILE_R, win_cols).astype(BF16)
        sums = sums + dot(place[:, 0 : spill_group * TILE_R], part)
    result_ref[0:owned_rows, :] = sums / jnp.maximum(total, 1.0)


def hand_over(result_ref, coadd_ref, weight_ref):
    owned_rows = coadd_ref.shape[0]
    coadd_ref[...] = result_ref[0:owned_rows, :]
    weight_ref[...] = result_ref[owned_rows : owned_rows + 1, :]


def on_device(
    image,
    row_taps,
    col_taps,
    mix_coeff,
    shift_frac,
    ccd_visit,
    visit_weight,
    tile_block,
    tile_offset,
):
    sky = lax.axis_size("sky")
    win_rows, win_cols = image.shape[1:]
    tiles = tile_block.shape[0]
    span = max(2, tiles // sky) * TILE_R
    owned_rows = BLK_DEV * TILE_R
    inputs = (
        image[0],
        row_taps.T,
        col_taps.T,
        mix_coeff.transpose(1, 0, 2),
        shift_frac,
        ccd_visit.reshape(1, 1),
        visit_weight.reshape(1, -1),
        tile_block.reshape(1, -1),
        tile_offset.reshape(1, -1),
    )
    vmem = pl.BlockSpec(memory_space=pltpu.VMEM)
    result = pl.pallas_call(
        functools.partial(kernel, sky),
        out_shape=pltpu.VMEM((owned_rows + 8, win_cols), F32),
        in_specs=[pl.BlockSpec(memory_space=pl.ANY)] * 9,
        out_specs=vmem,
        scratch_shapes=[
            *[pltpu.VMEM(value.shape, value.dtype) for value in inputs],
            pltpu.VMEM((win_rows + 72, win_cols), F32),
            pltpu.VMEM((2, win_rows // 2 + 32, LANES), F32),
            pltpu.VMEM((2, win_rows // 2 + 32, LANES), F32),
            pltpu.VMEM((2, win_rows // 2 + 16, LANES), F32),
            pltpu.VMEM((2, (row_taps.shape[1] + 2) * win_cols // 2, LANES), BF16),
            pltpu.VMEM((2, (row_taps.shape[1] + 2) * 16, LANES), BF16),
            pltpu.VMEM((sky * (span // 2 + 2 * TILE_R), tiles * TILE_R // 2), BF16),
            pltpu.VMEM((2, 32, LANES), F32),
            pltpu.VMEM((2, win_rows // 2, 2 * LANES), F32),
            pltpu.VMEM((2, win_rows // 2 + 16, win_cols), F32),
            pltpu.VMEM((sky, span + 2 * TILE_R, win_cols), BF16),
            pltpu.VMEM((sky, span + 2 * TILE_R, win_cols), BF16),
            pltpu.SemaphoreType.DMA((9,)),
            pltpu.SemaphoreType.DMA,
            pltpu.SemaphoreType.DMA,
        ],
        compiler_params=pltpu.CompilerParams(collective_id=0, has_side_effects=True),
        name="coadd",
    )(*inputs)
    coadd, weight_map = pl.pallas_call(
        hand_over,
        out_shape=(
            jax.ShapeDtypeStruct((owned_rows, win_cols), F32),
            jax.ShapeDtypeStruct((1, owned_rows), F32),
        ),
        in_specs=[vmem],
        out_specs=(vmem, vmem),
        name="hand_over",
    )(pltpu.with_memory_space_constraint(result, pltpu.VMEM))
    return coadd, weight_map.reshape(owned_rows)


def solution(mesh):
    return jax.shard_map(
        on_device,
        mesh=mesh,
        in_specs=(
            P(("groups", "sky"), None, None),
            P(),
            P(),
            P(("groups", "sky"), None, None),
            P(("groups", "sky"), None),
            P(("groups", "sky")),
            P("groups"),
            P(("groups", "sky")),
            P(("groups", "sky")),
        ),
        out_specs=(P(("groups", "sky"), None), P(("groups", "sky"))),
        check_vma=False,
    )
```

```python
import functools

import jax
import jax.numpy as jnp
from jax import lax
from jax.experimental import pallas as pl
from jax.experimental.pallas import tpu as pltpu
from jax.sharding import PartitionSpec as P

TILE_R = 8
BLK_DEV = 16
LANES = 128
F32 = jnp.float32
BF16 = jnp.bfloat16


def iota(shape, axis):
    return lax.broadcasted_iota(jnp.int32, shape, axis)


def dot(lhs, rhs):
    return jnp.dot(lhs, rhs, preferred_element_type=F32)


def onehot(mask):
    return jnp.where(mask, 1.0, 0.0).astype(BF16)


def lanczos(fraction):
    lane = iota((1, LANES), 1)
    offsets = (lane - 2).astype(F32) - fraction
    offsets = jnp.where(lane < 6, offsets, 0.5)
    angles = jnp.pi * offsets
    thirds = angles / 3.0
    kernel = jnp.sin(angles) / angles * (jnp.sin(thirds) / thirds)
    kernel = jnp.where(lane < 6, kernel, 0.0)
    return kernel / jnp.sum(kernel, axis=1, keepdims=True)


def kernel(
    sky,
    *refs,
):
    sources = refs[0:9]
    result_ref = refs[9]
    (
        image_ref,
        row_taps_ref,
        col_taps_ref,
        mix_ref,
        shift_ref,
        visit_ref,
        visit_weight_ref,
        block_ref,
        offset_ref,
    ) = held = refs[10:19]
    (
        xpad,
        pairs,
        edges,
        quads,
        body,
        rim,
        pick,
        taps2d,
        seeds,
        acc,
        spread_pad,
        data_send,
        data_recv,
        load_sem,
        data_ssem,
        data_rsem,
    ) = refs[19:]
    loads = [
        pltpu.make_async_copy(source, target, load_sem.at[number])
        for number, (source, target) in enumerate(zip(sources, held))
    ]
    for number in (1, 2, 3, 0, 7, 8, 5, 6, 4):
        loads[number].start()
    me = lax.axis_index("sky")
    win_rows, win_cols = image_ref.shape
    tap_count, basis = row_taps_ref.shape
    half = tap_count // 2
    tiles = block_ref.shape[1]
    cap = max(2, tiles // sky)
    span = cap * TILE_R
    owned_rows = BLK_DEV * TILE_R
    blk_shift = BLK_DEV.bit_length() - 1

    barrier = pltpu.get_barrier_semaphore()

    def greet(step, carry):
        pl.semaphore_signal(
            barrier,
            inc=1,
            device_id={"sky": lax.rem(me + step, sky)},
            device_id_type=pl.DeviceIdType.MESH,
        )
        return carry

    lax.fori_loop(1, sky, greet, 0)

    xpad[0:16, :] = jnp.zeros((16, win_cols), F32)
    xpad[win_rows + 16 :, :] = jnp.zeros((xpad.shape[0] - win_rows - 16, win_cols), F32)
    for number in (1, 2, 3):
        loads[number].wait()

    def message(send, recv, ssem, rsem, turn):
        to = turn - 1 + lax.div(turn - 1 - me + sky, jnp.int32(sky))
        return pltpu.make_async_remote_copy(
            src_ref=send.at[to],
            dst_ref=recv.at[me],
            send_sem=ssem,
            recv_sem=rsem,
            device_id={"sky": to},
            device_id_type=pl.DeviceIdType.MESH,
        )

    def wait_all(send, recv, ssem, rsem):
        copy = pltpu.make_async_remote_copy(
            src_ref=send.at[pl.ds(0, sky - 1)],
            dst_ref=recv.at[pl.ds(0, sky - 1)],
            send_sem=ssem,
            recv_sem=rsem,
            device_id={"sky": lax.rem(me + 1, sky)},
            device_id_type=pl.DeviceIdType.MESH,
        )
        copy.wait_send()
        copy.wait_recv()

    tap = iota((tap_count, 2 * LANES), 0)
    spot = iota((tap_count, 2 * LANES), 1)
    place = jnp.where(spot < LANES, 0, LANES // 2)
    flip = onehot(
        lax.rem(spot, jnp.int32(LANES)) == lax.rem(half + place - tap + LANES, jnp.int32(LANES))
    )
    flipped = lax.dot_general(
        row_taps_ref[...], flip, (((0,), (0,)), ((), ())), preferred_element_type=F32
    ).astype(BF16)
    near, far = flipped[:, 0:LANES], flipped[:, LANES:]

    def mixed(term, taps):
        value = col_taps_ref[...].astype(F32) * mix_ref[term]
        high = value.astype(BF16)
        low = (value - high.astype(F32)).astype(BF16)
        return dot(high, taps) + dot(low, taps)

    taps2d[0, 0:tap_count, :] = mixed(0, near) + mixed(2, far)
    taps2d[1, 0:tap_count, :] = mixed(1, near)

    side = win_cols // 2
    edge = 16
    pair_rows = win_rows // 2
    shifts = (tap_count + 1) // 2
    eight = (TILE_R, LANES)
    group = (edge, LANES)
    lane_of = iota(eight, 1)
    signed = lax.rem(lane_of + side, jnp.int32(LANES)) - side
    column_pos = (2.0 * signed.astype(F32) + 1.0) / win_cols - 1.0
    in_side = lax.rem(iota(group, 1), jnp.int32(side))
    inside = {
        first: onehot(jnp.abs(iota(group, 0) + first - in_side) <= half)
        for first in range(-edge, side + edge, edge)
        if first < half or first + edge + half > side
    }

    def slanted(tap):
        fixed, slope = (
            pltpu.roll(
                jnp.broadcast_to(taps2d[term, tap : tap + 1, :], eight),
                0,
                1,
                stride=1,
                stride_axis=0,
            )
            for term in range(2)
        )
        seeds[tap, 0:8, :] = fixed + column_pos * slope
        seeds[tap, 16:24, :] = slope

    def doubled(tap):
        fixed, slope = seeds[tap, 0:8, :], seeds[tap, 16:24, :]
        seeds[tap, 8:16, :] = pltpu.roll(fixed + (2.0 * TILE_R / win_cols) * slope, TILE_R, 1)
        seeds[tap, 24:32, :] = pltpu.roll(slope, TILE_R, 1)

    def toeplitz(tap):
        value = seeds[tap, 0:16, :]
        step = (2.0 * edge / win_cols) * seeds[tap, 16:32, :]
        for column in range(0, win_cols, edge):
            rounded = value.astype(BF16)
            for part in range(2):
                first = column - side * part
                if -edge * part <= first < side + edge * (1 - part):
                    rows = pltpu.roll(rounded, first % LANES, 1) if first else rounded
                    if first in inside:
                        rows = rows * inside[first]
                    if 0 <= first < side:
                        row = (tap + 1) * side + first
                        body[part, row : row + edge, :] = rows
                    else:
                        row = (tap + 1) * edge
                        rim[part, row : row + edge, :] = rows
            value = value + step

    for tap in range(tap_count):
        slanted(tap)
    for tap in range(tap_count):
        doubled(tap)

    for part in range(2):
        for row in (0, (tap_count + 1) * side):
            body[part, row : row + side, :] = jnp.zeros((side, LANES), BF16)
        for row in (0, (tap_count + 1) * edge):
            rim[part, row : row + edge, :] = jnp.zeros(group, BF16)

    for tap in range(0):
        toeplitz(tap)
    for number in (4, 5, 6, 7, 8, 0):
        loads[number].wait()
    xpad[pl.ds(16, win_rows), :] = image_ref[...].astype(F32)
    held_rows = pairs.shape[1]
    lane_of = iota((held_rows, LANES), 1)
    low = onehot(lane_of < side)
    high = onehot(lane_of >= side)
    odd = xpad[pl.ds(1, held_rows, stride=2), :].astype(BF16)
    even = xpad[pl.ds(2, held_rows, stride=2), :].astype(BF16)
    west = odd * low + pltpu.roll(even, side, 1) * high
    east = pltpu.roll(odd, side, 1) * low + even * high
    pairs[0] = west.astype(F32)
    pairs[1] = east.astype(F32)

    for tap in range(0, tap_count):
        toeplitz(tap)

    block = block_ref[...]
    owner_i = lax.shift_right_logical(block, blk_shift)
    start_row = ((block - owner_i * BLK_DEV) * TILE_R + offset_ref[...]).astype(F32)
    owner_row = owner_i.astype(F32)
    eye = iota((tiles, tiles), 0) == iota((tiles, tiles), 1)
    column = lambda row: jnp.sum(
        jnp.where(eye, jnp.broadcast_to(row, (tiles, tiles)), 0.0), axis=1, keepdims=True
    )
    owner_col = column(owner_row)
    start_col = column(start_row)
    same = owner_col == owner_row
    below = iota((tiles, tiles), 0) < iota((tiles, tiles), 1)
    above = iota((tiles, tiles), 1) < iota((tiles, tiles), 0)
    rank_row = jnp.sum(jnp.where(same & below, 1.0, 0.0), axis=0, keepdims=True)
    rank_col = jnp.sum(jnp.where(same & above, 1.0, 0.0), axis=1, keepdims=True)
    visits = visit_weight_ref.shape[1]
    own_weight = jnp.sum(
        jnp.where(
            iota((1, visits), 1) == visit_ref[...], visit_weight_ref[...].astype(F32), 0.0
        ),
        axis=1,
        keepdims=True,
    )

    per_group = LANES // span
    spill_group = min(LANES // TILE_R, sky)
    sub = iota((sky * TILE_R, tiles), 0)
    owner_of = lax.shift_right_logical(sub, 3).astype(F32)
    lane = iota((tiles, LANES), 1)
    mine = lax.div(lane, jnp.int32(span)) == lax.rem(me, per_group)
    local = lax.rem(lane, jnp.int32(span))
    parity = lax.div(local, jnp.int32(span // 2))
    local = lax.rem(local, jnp.int32(span // 2))
    slot_rank = lax.div(local, jnp.int32(TILE_R // 2)).astype(F32)
    in_eight = (2 * lax.rem(local, jnp.int32(TILE_R // 2)) + parity).astype(F32)
    landing = jnp.where(mine & (slot_rank == rank_col), start_col + in_eight + 1.0, 0.0)
    in_eight = lax.rem(lane, jnp.int32(TILE_R)).astype(F32)
    targets = dot(onehot(owner_of == owner_row), landing.astype(BF16))
    mine = lax.div(lane, jnp.int32(TILE_R)) == lax.rem(me, spill_group)
    cover = onehot(mine & (start_col > in_eight + float(owned_rows - TILE_R)))
    covered = dot(onehot(owner_of - 1.0 == owner_row), cover)
    lane8 = iota((sky * TILE_R, LANES), 1)
    sub8 = lax.rem(iota((sky * TILE_R, LANES), 0), jnp.int32(TILE_R))
    weight8 = jnp.broadcast_to(own_weight, (sky * TILE_R, LANES))
    tile_lanes = lax.div(lane8, jnp.int32(span)) == lax.rem(me, per_group)
    spill_lanes = lax.div(lane8, jnp.int32(TILE_R)) == lax.rem(me, spill_group)
    header = jnp.where((sub8 == 1) & tile_lanes, weight8, 0.0)
    header = jnp.where((sub8 == 2) & spill_lanes, weight8, header)
    header = jnp.where(sub8 == 3, covered, header)
    header = jnp.where(sub8 == 0, targets, header)
    data_send[:, span + TILE_R :, :] = header.reshape(sky, TILE_R, LANES).astype(BF16)

    wide = tiles * TILE_R // 2
    widen = onehot(
        iota((tiles, wide), 0) == lax.shift_right_logical(iota((tiles, wide), 1), 2)
    )
    in_tile = (2 * lax.rem(iota((1, wide), 1), jnp.int32(TILE_R // 2))).astype(F32)
    spread8 = lambda row: dot(jnp.broadcast_to(row, (8, tiles)).astype(BF16), widen)[0:1, :]
    owner_wide = spread8(owner_row)
    slot_lane = spread8(owner_row * cap + rank_row) * (TILE_R // 2) + in_tile / 2.0
    sent = sky * span // 2
    past = spread8(start_row) + in_tile - float(owned_rows)
    pick[0:sent, :] = onehot(iota((sent, wide), 0).astype(F32) == slot_lane)
    spills = sky * TILE_R
    for parity in range(2):
        moved = past + float(parity)
        spill_lane = jnp.where(moved >= 0.0, (owner_wide + 1.0) * TILE_R + moved, -1.0)
        pick[sent + parity * spills : sent + (parity + 1) * spills, :] = onehot(
            iota((spills, wide), 0).astype(F32) == spill_lane
        )

    low = onehot(lane_of < edge)
    high = onehot((lane_of >= edge) & (lane_of < 2 * edge))
    quad_rows = quads.shape[1]
    quarter = lax.div(iota((quad_rows, LANES), 1), jnp.int32(2 * edge))
    for part in range(2):
        if part:
            strip = pltpu.roll(west, edge + side, 1) * low + pltpu.roll(west, 2 * edge, 1) * high
        else:
            strip = east * low + pltpu.roll(east, edge + side, 1) * high
        strip = strip + pltpu.roll(strip, 2 * edge, 1)
        strip = strip + pltpu.roll(strip, 4 * edge, 1)
        edges[part] = strip.astype(F32)
        value = edges[part, 0:quad_rows, :]
        for later in range(1, 4):
            value = jnp.where(quarter == later, edges[part, pl.ds(later, quad_rows), :], value)
        quads[part] = value

    def product(part):
        left = [pairs[part, pl.ds(shift, pair_rows), :].astype(BF16) for shift in range(shifts)]
        left += [
            quads[part, pl.ds(first, pair_rows), :].astype(BF16) for first in range(0, shifts, 4)
        ]
        last, far = (tap_count + 1) * side, (tap_count + 1) * edge
        early = jnp.concatenate([body[part, side : last + side, :], rim[part, edge : far + edge, :]], axis=0)
        late = jnp.concatenate([body[part, 0:last, :], rim[part, 0:far, :]], axis=0)
        return dot(jnp.concatenate(left, axis=1), jnp.concatenate([early, late], axis=1))

    for part in range(2):
        acc[part] = product(part)

    across = lanczos(shift_ref[0:1, 1:2])
    down = lanczos(shift_ref[0:1, 0:1])
    chunk = min(64, pair_rows)
    for parity in range(2):
        spread_pad[parity, 0:8, :] = jnp.zeros((8, win_cols), F32)
        spread_pad[parity, pair_rows + 8 :, :] = jnp.zeros((8, win_cols), F32)
    down_taps = [
        jnp.broadcast_to(down[0:1, m + 2 : m + 3], (1, win_cols)) for m in range(-2, 4)
    ]
    square = (2 * LANES, LANES)
    pixel = lax.div(iota(square, 0), jnp.int32(LANES)) * side + lax.rem(
        iota(square, 0), jnp.int32(side)
    )
    warp = jnp.zeros(square, F32)
    for m in range(-2, 4):
        warp = jnp.where(pixel - iota(square, 1) == m, across[0:1, m + 2 : m + 3], warp)
    warp_high = warp.astype(BF16)
    warp_low = (warp - warp_high.astype(F32)).astype(BF16)
    warp_both = jnp.concatenate([warp_high, warp_low], axis=1)
    in_first = iota((chunk, LANES), 1) < side
    for first in range(0, pair_rows, chunk):
        here = slice(first, first + chunk)
        for parity in range(2):
            columns = slice(parity * LANES, (parity + 1) * LANES)
            row_pos = (2 * (iota((chunk, LANES), 0) + first) + parity).astype(F32)
            row_pos = (2.0 * row_pos + 1.0) / win_rows - 1.0
            factor = jnp.where(in_first, 1.0, row_pos)
            terms = jnp.concatenate(
                [acc[0, here, columns] * factor, acc[1, here, columns] * factor], axis=1
            )
            high = terms.astype(BF16)
            low = (terms - high.astype(F32)).astype(BF16)
            both = dot(high, warp_both)
            spread = both[:, 0:LANES] + both[:, LANES:] + dot(low, warp_high)
            spread_pad[parity, first + 8 : first + 8 + chunk, :] = spread
    warped = []
    for parity in range(2):
        rows = []
        for first in range(0, pair_rows, chunk):
            value = None
            for m in range(-2, 4):
                other = (parity + m) % 2
                down_by = (parity + m - other) // 2
                term = down_taps[m + 2] * spread_pad[other, pl.ds(first + 8 + down_by, chunk), :]
                value = term if value is None else value + term
            rows.append(value.astype(BF16))
        warped.append(jnp.concatenate(rows, axis=0))
    warped = jnp.concatenate(warped, axis=1)

    packed = dot(pick[...], warped)
    tile_rows = (sky, span // 2, win_cols)
    tile_rows = [packed[0:sent, columns].reshape(tile_rows) for columns in (slice(0, LANES), slice(LANES, 2 * LANES))]
    data_send[:, 0:span, :] = jnp.concatenate(tile_rows, axis=1).astype(BF16)
    spilled = packed[sent : sent + spills, 0:LANES] + packed[sent + spills :, LANES:]
    data_send[:, span : span + TILE_R, :] = spilled.reshape(sky, TILE_R, win_cols).astype(BF16)

    def start_data(step, carry):
        message(data_send, data_recv, data_ssem, data_rsem, step).start()
        return carry

    pl.semaphore_wait(barrier, sky - 1)
    lax.fori_loop(1, sky, start_data, 0)
    data_recv[pl.ds(me, 1)] = data_send[pl.ds(me, 1)]

    wait_all(data_send, data_recv, data_ssem, data_rsem)

    owned = (owned_rows, LANES)
    row_id = (iota(owned, 0) + 1).astype(F32)
    places = []
    total = jnp.zeros((owned_rows, win_cols), F32)
    ones = jnp.ones((LANES, win_cols), BF16)
    for group in range(sky // per_group):
        head = data_recv[group * per_group : (group + 1) * per_group, span + TILE_R :, :]
        head = jnp.sum(head.astype(F32), axis=0)
        place = jnp.where(head[0:1, :] == row_id, head[1:2, :], 0.0).astype(BF16)
        places.append(place)
        total = total + dot(place, ones)
    spill_places = []
    same_row = lax.rem(iota(owned, 1), jnp.int32(TILE_R)) == iota(owned, 0)
    here_row = lax.rem(iota(eight, 1), jnp.int32(TILE_R)) == iota(eight, 0)
    first_rows = jnp.zeros(eight, F32)
    for group in range(sky // spill_group):
        head = data_recv[group * spill_group : (group + 1) * spill_group, span + TILE_R :, :]
        head = jnp.sum(head.astype(F32), axis=0)
        spill_places.append(jnp.where(same_row, head[2:3, :], 0.0).astype(BF16))
        count = jnp.sum(jnp.where(here_row, head[2:3, :] * head[3:4, :], 0.0), axis=1, keepdims=True)
        first_rows = first_rows + jnp.broadcast_to(count, eight)
    total = total + jnp.concatenate(
        [first_rows, jnp.zeros((owned_rows - TILE_R, LANES), F32)], axis=0
    )
    diagonal = iota(owned, 0) == iota(owned, 1)
    result_ref[owned_rows:, :] = jnp.broadcast_to(
        jnp.sum(jnp.where(diagonal, total, 0.0), axis=0, keepdims=True), (8, LANES)
    )

    sums = jnp.zeros((owned_rows, win_cols), F32)
    for group, place in enumerate(places):
        part = data_recv[group * per_group : (group + 1) * per_group, 0:span, :]
        sums = sums + dot(place, part.reshape(LANES, win_cols))
    for group, place in enumerate(spill_places):
        part = data_recv[group * spill_group : (group + 1) * spill_group, span : span + TILE_R, :]
        part = part.astype(F32).reshape(spill_group * TILE_R, win_cols).astype(BF16)
        sums = sums + dot(place[:, 0 : spill_group * TILE_R], part)
    result_ref[0:owned_rows, :] = sums / jnp.maximum(total, 1.0)


def hand_over(result_ref, coadd_ref, weight_ref):
    owned_rows = coadd_ref.shape[0]
    coadd_ref[...] = result_ref[0:owned_rows, :]
    weight_ref[...] = result_ref[owned_rows : owned_rows + 1, :]


def on_device(
    image,
    row_taps,
    col_taps,
    mix_coeff,
    shift_frac,
    ccd_visit,
    visit_weight,
    tile_block,
    tile_offset,
):
    sky = lax.axis_size("sky")
    win_rows, win_cols = image.shape[1:]
    tiles = tile_block.shape[0]
    span = max(2, tiles // sky) * TILE_R
    owned_rows = BLK_DEV * TILE_R
    inputs = (
        image[0],
        row_taps.T,
        col_taps.T,
        mix_coeff.transpose(1, 0, 2),
        shift_frac,
        ccd_visit.reshape(1, 1),
        visit_weight.reshape(1, -1),
        tile_block.reshape(1, -1),
        tile_offset.reshape(1, -1),
    )
    vmem = pl.BlockSpec(memory_space=pltpu.VMEM)
    result = pl.pallas_call(
        functools.partial(kernel, sky),
        out_shape=pltpu.VMEM((owned_rows + 8, win_cols), F32),
        in_specs=[pl.BlockSpec(memory_space=pl.ANY)] * 9,
        out_specs=vmem,
        scratch_shapes=[
            *[pltpu.VMEM(value.shape, value.dtype) for value in inputs],
            pltpu.VMEM((win_rows + 72, win_cols), F32),
            pltpu.VMEM((2, win_rows // 2 + 32, LANES), F32),
            pltpu.VMEM((2, win_rows // 2 + 32, LANES), F32),
            pltpu.VMEM((2, win_rows // 2 + 16, LANES), F32),
            pltpu.VMEM((2, (row_taps.shape[1] + 2) * win_cols // 2, LANES), BF16),
            pltpu.VMEM((2, (row_taps.shape[1] + 2) * 16, LANES), BF16),
            pltpu.VMEM((sky * (span // 2 + 2 * TILE_R), tiles * TILE_R // 2), BF16),
            pltpu.VMEM((2, 32, LANES), F32),
            pltpu.VMEM((row_taps.shape[1], 32, LANES), F32),
            pltpu.VMEM((2, win_rows // 2, 2 * LANES), F32),
            pltpu.VMEM((2, win_rows // 2 + 16, win_cols), F32),
            pltpu.VMEM((sky, span + 2 * TILE_R, win_cols), BF16),
            pltpu.VMEM((sky, span + 2 * TILE_R, win_cols), BF16),
            pltpu.SemaphoreType.DMA((9,)),
            pltpu.SemaphoreType.DMA,
            pltpu.SemaphoreType.DMA,
        ],
        compiler_params=pltpu.CompilerParams(collective_id=0, has_side_effects=True),
        name="coadd",
    )(*inputs)
    coadd, weight_map = pl.pallas_call(
        hand_over,
        out_shape=(
            jax.ShapeDtypeStruct((owned_rows, win_cols), F32),
            jax.ShapeDtypeStruct((1, owned_rows), F32),
        ),
        in_specs=[vmem],
        out_specs=(vmem, vmem),
        name="hand_over",
    )(pltpu.with_memory_space_constraint(result, pltpu.VMEM))
    return coadd, weight_map.reshape(owned_rows)


def solution(mesh):
    return jax.shard_map(
        on_device,
        mesh=mesh,
        in_specs=(
            P(("groups", "sky"), None, None),
            P(),
            P(),
            P(("groups", "sky"), None, None),
            P(("groups", "sky"), None),
            P(("groups", "sky")),
            P("groups"),
            P(("groups", "sky")),
            P(("groups", "sky")),
        ),
        out_specs=(P(("groups", "sky"), None), P(("groups", "sky"))),
        check_vma=False,
    )
```

```python
import functools

import jax
import jax.numpy as jnp
from jax import lax
from jax.experimental import pallas as pl
from jax.experimental.pallas import tpu as pltpu
from jax.sharding import PartitionSpec as P

TILE_R = 8
BLK_DEV = 16
LANES = 128
F32 = jnp.float32
BF16 = jnp.bfloat16


def iota(shape, axis):
    return lax.broadcasted_iota(jnp.int32, shape, axis)


def dot(lhs, rhs):
    return jnp.dot(lhs, rhs, preferred_element_type=F32)


def onehot(mask):
    return jnp.where(mask, 1.0, 0.0).astype(BF16)


def lanczos(fraction):
    lane = iota((1, LANES), 1)
    offsets = (lane - 2).astype(F32) - fraction
    offsets = jnp.where(lane < 6, offsets, 0.5)
    angles = jnp.pi * offsets
    thirds = angles / 3.0
    kernel = jnp.sin(angles) / angles * (jnp.sin(thirds) / thirds)
    kernel = jnp.where(lane < 6, kernel, 0.0)
    return kernel / jnp.sum(kernel, axis=1, keepdims=True)


def kernel(
    sky,
    *refs,
):
    sources = refs[0:9]
    result_ref = refs[9]
    (
        image_ref,
        row_taps_ref,
        col_taps_ref,
        mix_ref,
        shift_ref,
        visit_ref,
        visit_weight_ref,
        block_ref,
        offset_ref,
    ) = held = refs[10:19]
    (
        xpad,
        pairs,
        edges,
        quads,
        body,
        rim,
        pick,
        taps2d,
        seeds,
        acc,
        spread_pad,
        data_send,
        data_recv,
        load_sem,
        data_ssem,
        data_rsem,
    ) = refs[19:]
    loads = [
        pltpu.make_async_copy(source, target, load_sem.at[number])
        for number, (source, target) in enumerate(zip(sources, held))
    ]
    for number in (1, 2, 3, 0, 7, 8, 5, 6, 4):
        loads[number].start()
    me = lax.axis_index("sky")
    win_rows, win_cols = image_ref.shape
    tap_count, basis = row_taps_ref.shape
    half = tap_count // 2
    tiles = block_ref.shape[1]
    cap = max(2, tiles // sky)
    span = cap * TILE_R
    owned_rows = BLK_DEV * TILE_R
    blk_shift = BLK_DEV.bit_length() - 1

    per_group = LANES // span
    spill_group = min(LANES // TILE_R, sky)
    barrier = pltpu.get_barrier_semaphore()

    def greet(step, carry):
        pl.semaphore_signal(
            barrier,
            inc=1,
            device_id={"sky": lax.rem(me + step, sky)},
            device_id_type=pl.DeviceIdType.MESH,
        )
        return carry

    lax.fori_loop(1, sky, greet, 0)

    xpad[0:16, :] = jnp.zeros((16, win_cols), F32)
    xpad[win_rows + 16 :, :] = jnp.zeros((xpad.shape[0] - win_rows - 16, win_cols), F32)
    for number in (1, 2, 3):
        loads[number].wait()

    def message(turn):
        to = turn - 1 + lax.div(turn - 1 - me + sky, jnp.int32(sky))
        return pltpu.make_async_remote_copy(
            src_ref=data_send.at[to],
            dst_ref=data_recv.at[me],
            send_sem=data_ssem,
            recv_sem=data_rsem,
            device_id={"sky": to},
            device_id_type=pl.DeviceIdType.MESH,
        )

    def arrivals(count):
        return pltpu.make_async_remote_copy(
            src_ref=data_send.at[pl.ds(0, count)],
            dst_ref=data_recv.at[pl.ds(0, count)],
            send_sem=data_ssem,
            recv_sem=data_rsem,
            device_id={"sky": lax.rem(me + 1, sky)},
            device_id_type=pl.DeviceIdType.MESH,
        )

    tap = iota((tap_count, 2 * LANES), 0)
    spot = iota((tap_count, 2 * LANES), 1)
    place = jnp.where(spot < LANES, 0, LANES // 2)
    flip = onehot(
        lax.rem(spot, jnp.int32(LANES)) == lax.rem(half + place - tap + LANES, jnp.int32(LANES))
    )
    flipped = lax.dot_general(
        row_taps_ref[...], flip, (((0,), (0,)), ((), ())), preferred_element_type=F32
    ).astype(BF16)
    near, far = flipped[:, 0:LANES], flipped[:, LANES:]

    def mixed(term, taps):
        value = col_taps_ref[...].astype(F32) * mix_ref[term]
        high = value.astype(BF16)
        low = (value - high.astype(F32)).astype(BF16)
        return dot(high, taps) + dot(low, taps)

    taps2d[0, 0:tap_count, :] = mixed(0, near) + mixed(2, far)
    taps2d[1, 0:tap_count, :] = mixed(1, near)

    side = win_cols // 2
    edge = 16
    pair_rows = win_rows // 2
    shifts = (tap_count + 1) // 2
    eight = (TILE_R, LANES)
    group = (edge, LANES)
    lane_of = iota(eight, 1)
    signed = lax.rem(lane_of + side, jnp.int32(LANES)) - side
    column_pos = (2.0 * signed.astype(F32) + 1.0) / win_cols - 1.0
    in_side = lax.rem(iota(group, 1), jnp.int32(side))
    inside = {
        first: onehot(jnp.abs(iota(group, 0) + first - in_side) <= half)
        for first in range(-edge, side + edge, edge)
        if first < half or first + edge + half > side
    }

    def slanted(tap):
        fixed, slope = (
            pltpu.roll(
                jnp.broadcast_to(taps2d[term, tap : tap + 1, :], eight),
                0,
                1,
                stride=1,
                stride_axis=0,
            )
            for term in range(2)
        )
        seeds[tap, 0:8, :] = fixed + column_pos * slope
        seeds[tap, 16:24, :] = slope

    def doubled(tap):
        fixed, slope = seeds[tap, 0:8, :], seeds[tap, 16:24, :]
        seeds[tap, 8:16, :] = pltpu.roll(fixed + (2.0 * TILE_R / win_cols) * slope, TILE_R, 1)
        seeds[tap, 24:32, :] = pltpu.roll(slope, TILE_R, 1)

    def toeplitz(tap):
        value = seeds[tap, 0:16, :]
        step = (2.0 * edge / win_cols) * seeds[tap, 16:32, :]
        for column in range(0, win_cols, edge):
            rounded = value.astype(BF16)
            for part in range(2):
                first = column - side * part
                if -edge * part <= first < side + edge * (1 - part):
                    rows = pltpu.roll(rounded, first % LANES, 1) if first else rounded
                    if first in inside:
                        rows = rows * inside[first]
                    if 0 <= first < side:
                        row = (tap + 1) * side + first
                        body[part, row : row + edge, :] = rows
                    else:
                        row = (tap + 1) * edge
                        rim[part, row : row + edge, :] = rows
            value = value + step

    for tap in range(tap_count):
        slanted(tap)
    for tap in range(tap_count):
        doubled(tap)

    for part in range(2):
        for row in (0, (tap_count + 1) * side):
            body[part, row : row + side, :] = jnp.zeros((side, LANES), BF16)
        for row in (0, (tap_count + 1) * edge):
            rim[part, row : row + edge, :] = jnp.zeros(group, BF16)

    for tap in range(0):
        toeplitz(tap)
    for number in (4, 5, 6, 7, 8, 0):
        loads[number].wait()
    xpad[pl.ds(16, win_rows), :] = image_ref[...].astype(F32)
    held_rows = pairs.shape[1]
    lane_of = iota((held_rows, LANES), 1)
    low = onehot(lane_of < side)
    high = onehot(lane_of >= side)
    odd = xpad[pl.ds(1, held_rows, stride=2), :].astype(BF16)
    even = xpad[pl.ds(2, held_rows, stride=2), :].astype(BF16)
    west = odd * low + pltpu.roll(even, side, 1) * high
    east = pltpu.roll(odd, side, 1) * low + even * high
    pairs[0] = west.astype(F32)
    pairs[1] = east.astype(F32)

    for tap in range(0, tap_count):
        toeplitz(tap)

    block = block_ref[...]
    owner_i = lax.shift_right_logical(block, blk_shift)
    start_row = ((block - owner_i * BLK_DEV) * TILE_R + offset_ref[...]).astype(F32)
    owner_row = owner_i.astype(F32)
    eye = iota((tiles, tiles), 0) == iota((tiles, tiles), 1)
    column = lambda row: jnp.sum(
        jnp.where(eye, jnp.broadcast_to(row, (tiles, tiles)), 0.0), axis=1, keepdims=True
    )
    owner_col = column(owner_row)
    start_col = column(start_row)
    same = owner_col == owner_row
    below = iota((tiles, tiles), 0) < iota((tiles, tiles), 1)
    above = iota((tiles, tiles), 1) < iota((tiles, tiles), 0)
    rank_row = jnp.sum(jnp.where(same & below, 1.0, 0.0), axis=0, keepdims=True)
    rank_col = jnp.sum(jnp.where(same & above, 1.0, 0.0), axis=1, keepdims=True)
    visits = visit_weight_ref.shape[1]
    own_weight = jnp.sum(
        jnp.where(
            iota((1, visits), 1) == visit_ref[...], visit_weight_ref[...].astype(F32), 0.0
        ),
        axis=1,
        keepdims=True,
    )

    sub = iota((sky * TILE_R, tiles), 0)
    owner_of = lax.shift_right_logical(sub, 3).astype(F32)
    lane = iota((tiles, LANES), 1)
    mine = lax.div(lane, jnp.int32(span)) == lax.rem(me, per_group)
    local = lax.rem(lane, jnp.int32(span))
    parity = lax.div(local, jnp.int32(span // 2))
    local = lax.rem(local, jnp.int32(span // 2))
    slot_rank = lax.div(local, jnp.int32(TILE_R // 2)).astype(F32)
    in_eight = (2 * lax.rem(local, jnp.int32(TILE_R // 2)) + parity).astype(F32)
    landing = jnp.where(mine & (slot_rank == rank_col), start_col + in_eight + 1.0, 0.0)
    in_eight = lax.rem(lane, jnp.int32(TILE_R)).astype(F32)
    targets = dot(onehot(owner_of == owner_row), landing.astype(BF16))
    mine = lax.div(lane, jnp.int32(TILE_R)) == lax.rem(me, spill_group)
    cover = onehot(mine & (start_col > in_eight + float(owned_rows - TILE_R)))
    covered = dot(onehot(owner_of - 1.0 == owner_row), cover)
    lane8 = iota((sky * TILE_R, LANES), 1)
    sub8 = lax.rem(iota((sky * TILE_R, LANES), 0), jnp.int32(TILE_R))
    weight8 = jnp.broadcast_to(own_weight, (sky * TILE_R, LANES))
    tile_lanes = lax.div(lane8, jnp.int32(span)) == lax.rem(me, per_group)
    spill_lanes = lax.div(lane8, jnp.int32(TILE_R)) == lax.rem(me, spill_group)
    header = jnp.where((sub8 == 1) & tile_lanes, weight8, 0.0)
    header = jnp.where((sub8 == 2) & spill_lanes, weight8, header)
    header = jnp.where(sub8 == 3, covered, header)
    header = jnp.where(sub8 == 0, targets, header)
    data_send[:, span + TILE_R :, :] = header.reshape(sky, TILE_R, LANES).astype(BF16)

    wide = tiles * TILE_R // 2
    widen = onehot(
        iota((tiles, wide), 0) == lax.shift_right_logical(iota((tiles, wide), 1), 2)
    )
    in_tile = (2 * lax.rem(iota((1, wide), 1), jnp.int32(TILE_R // 2))).astype(F32)
    spread8 = lambda row: dot(jnp.broadcast_to(row, (8, tiles)).astype(BF16), widen)[0:1, :]
    owner_wide = spread8(owner_row)
    slot_lane = spread8(owner_row * cap + rank_row) * (TILE_R // 2) + in_tile / 2.0
    cuts = (0, sky // 4, sky // 2, sky)
    pick_rows = span // 2 + 2 * TILE_R
    past = spread8(start_row) + in_tile - float(owned_rows)
    spill_lanes = []
    for parity in range(2):
        moved = past + float(parity)
        spill_lanes.append(jnp.where(moved >= 0.0, (owner_wide + 1.0) * TILE_R + moved, -1.0))
    for first, last in zip(cuts, cuts[1:]):
        base = first * pick_rows
        for rows, lanes in ((span // 2, slot_lane), (TILE_R, spill_lanes[0]), (TILE_R, spill_lanes[1])):
            count = (last - first) * rows
            place = (iota((count, wide), 0) + first * rows).astype(F32)
            pick[base : base + count, :] = onehot(place == lanes)
            base += count

    low = onehot(lane_of < edge)
    high = onehot((lane_of >= edge) & (lane_of < 2 * edge))
    quad_rows = quads.shape[1]
    quarter = lax.div(iota((quad_rows, LANES), 1), jnp.int32(2 * edge))
    for part in range(2):
        if part:
            strip = pltpu.roll(west, edge + side, 1) * low + pltpu.roll(west, 2 * edge, 1) * high
        else:
            strip = east * low + pltpu.roll(east, edge + side, 1) * high
        strip = strip + pltpu.roll(strip, 2 * edge, 1)
        strip = strip + pltpu.roll(strip, 4 * edge, 1)
        edges[part] = strip.astype(F32)
        value = edges[part, 0:quad_rows, :]
        for later in range(1, 4):
            value = jnp.where(quarter == later, edges[part, pl.ds(later, quad_rows), :], value)
        quads[part] = value

    def product(part):
        left = [pairs[part, pl.ds(shift, pair_rows), :].astype(BF16) for shift in range(shifts)]
        left += [
            quads[part, pl.ds(first, pair_rows), :].astype(BF16) for first in range(0, shifts, 4)
        ]
        last, far = (tap_count + 1) * side, (tap_count + 1) * edge
        early = jnp.concatenate([body[part, side : last + side, :], rim[part, edge : far + edge, :]], axis=0)
        late = jnp.concatenate([body[part, 0:last, :], rim[part, 0:far, :]], axis=0)
        return dot(jnp.concatenate(left, axis=1), jnp.concatenate([early, late], axis=1))

    for part in range(2):
        acc[part] = product(part)

    across = lanczos(shift_ref[0:1, 1:2])
    down = lanczos(shift_ref[0:1, 0:1])
    chunk = min(64, pair_rows)
    for parity in range(2):
        spread_pad[parity, 0:8, :] = jnp.zeros((8, win_cols), F32)
        spread_pad[parity, pair_rows + 8 :, :] = jnp.zeros((8, win_cols), F32)
    down_taps = [
        jnp.broadcast_to(down[0:1, m + 2 : m + 3], (1, win_cols)) for m in range(-2, 4)
    ]
    square = (2 * LANES, LANES)
    pixel = lax.div(iota(square, 0), jnp.int32(LANES)) * side + lax.rem(
        iota(square, 0), jnp.int32(side)
    )
    warp = jnp.zeros(square, F32)
    for m in range(-2, 4):
        warp = jnp.where(pixel - iota(square, 1) == m, across[0:1, m + 2 : m + 3], warp)
    warp_high = warp.astype(BF16)
    warp_low = (warp - warp_high.astype(F32)).astype(BF16)
    warp_both = jnp.concatenate([warp_high, warp_low], axis=1)
    in_first = iota((chunk, LANES), 1) < side
    for first in range(0, pair_rows, chunk):
        here = slice(first, first + chunk)
        for parity in range(2):
            columns = slice(parity * LANES, (parity + 1) * LANES)
            row_pos = (2 * (iota((chunk, LANES), 0) + first) + parity).astype(F32)
            row_pos = (2.0 * row_pos + 1.0) / win_rows - 1.0
            factor = jnp.where(in_first, 1.0, row_pos)
            terms = jnp.concatenate(
                [acc[0, here, columns] * factor, acc[1, here, columns] * factor], axis=1
            )
            high = terms.astype(BF16)
            low = (terms - high.astype(F32)).astype(BF16)
            both = dot(high, warp_both)
            spread = both[:, 0:LANES] + both[:, LANES:] + dot(low, warp_high)
            spread_pad[parity, first + 8 : first + 8 + chunk, :] = spread
    warped = []
    for parity in range(2):
        rows = []
        for first in range(0, pair_rows, chunk):
            value = None
            for m in range(-2, 4):
                other = (parity + m) % 2
                down_by = (parity + m - other) // 2
                term = down_taps[m + 2] * spread_pad[other, pl.ds(first + 8 + down_by, chunk), :]
                value = term if value is None else value + term
            rows.append(value.astype(BF16))
        warped.append(jnp.concatenate(rows, axis=0))
    warped = jnp.concatenate(warped, axis=1)

    pl.semaphore_wait(barrier, sky - 1)
    for first, last in zip(cuts, cuts[1:]):
        packed = dot(pick[first * pick_rows : last * pick_rows, :], warped)
        count = last - first
        sent, spills = count * span // 2, count * TILE_R
        halves = [
            packed[0:sent, parity * LANES : (parity + 1) * LANES].reshape(count, span // 2, win_cols)
            for parity in range(2)
        ]
        data_send[first:last, 0:span, :] = jnp.concatenate(halves, axis=1).astype(BF16)
        spilled = packed[sent : sent + spills, 0:LANES] + packed[sent + spills :, LANES:]
        data_send[first:last, span : span + TILE_R, :] = spilled.reshape(
            count, TILE_R, win_cols
        ).astype(BF16)

        def start_data(step, carry):
            message(step).start()
            return carry

        lax.fori_loop(max(first, 1), last, start_data, 0)
    data_recv[pl.ds(me, 1)] = data_send[pl.ds(me, 1)]

    arrivals(sky - 1).wait_recv()

    owned = (owned_rows, LANES)
    row_id = (iota(owned, 0) + 1).astype(F32)
    places = []
    total = jnp.zeros((owned_rows, win_cols), F32)
    ones = jnp.ones((LANES, win_cols), BF16)
    for group in range(sky // per_group):
        head = data_recv[group * per_group : (group + 1) * per_group, span + TILE_R :, :]
        head = jnp.sum(head.astype(F32), axis=0)
        place = jnp.where(head[0:1, :] == row_id, head[1:2, :], 0.0).astype(BF16)
        places.append(place)
        total = total + dot(place, ones)
    spill_places = []
    same_row = lax.rem(iota(owned, 1), jnp.int32(TILE_R)) == iota(owned, 0)
    here_row = lax.rem(iota(eight, 1), jnp.int32(TILE_R)) == iota(eight, 0)
    first_rows = jnp.zeros(eight, F32)
    for group in range(sky // spill_group):
        head = data_recv[group * spill_group : (group + 1) * spill_group, span + TILE_R :, :]
        head = jnp.sum(head.astype(F32), axis=0)
        spill_places.append(jnp.where(same_row, head[2:3, :], 0.0).astype(BF16))
        count = jnp.sum(jnp.where(here_row, head[2:3, :] * head[3:4, :], 0.0), axis=1, keepdims=True)
        first_rows = first_rows + jnp.broadcast_to(count, eight)
    total = total + jnp.concatenate(
        [first_rows, jnp.zeros((owned_rows - TILE_R, LANES), F32)], axis=0
    )
    diagonal = iota(owned, 0) == iota(owned, 1)
    result_ref[owned_rows:, :] = jnp.broadcast_to(
        jnp.sum(jnp.where(diagonal, total, 0.0), axis=0, keepdims=True), (8, LANES)
    )

    sums = jnp.zeros((owned_rows, win_cols), F32)
    for group, place in enumerate(places):
        part = data_recv[group * per_group : (group + 1) * per_group, 0:span, :]
        sums = sums + dot(place, part.reshape(LANES, win_cols))
    for group, place in enumerate(spill_places):
        part = data_recv[group * spill_group : (group + 1) * spill_group, span : span + TILE_R, :]
        part = part.astype(F32).reshape(spill_group * TILE_R, win_cols).astype(BF16)
        sums = sums + dot(place[:, 0 : spill_group * TILE_R], part)
    result_ref[0:owned_rows, :] = sums / jnp.maximum(total, 1.0)
    arrivals(sky - 1).wait_send()


def hand_over(result_ref, coadd_ref, weight_ref):
    owned_rows = coadd_ref.shape[0]
    coadd_ref[...] = result_ref[0:owned_rows, :]
    weight_ref[...] = result_ref[owned_rows : owned_rows + 1, :]


def on_device(
    image,
    row_taps,
    col_taps,
    mix_coeff,
    shift_frac,
    ccd_visit,
    visit_weight,
    tile_block,
    tile_offset,
):
    sky = lax.axis_size("sky")
    win_rows, win_cols = image.shape[1:]
    tiles = tile_block.shape[0]
    span = max(2, tiles // sky) * TILE_R
    owned_rows = BLK_DEV * TILE_R
    inputs = (
        image[0],
        row_taps.T,
        col_taps.T,
        mix_coeff.transpose(1, 0, 2),
        shift_frac,
        ccd_visit.reshape(1, 1),
        visit_weight.reshape(1, -1),
        tile_block.reshape(1, -1),
        tile_offset.reshape(1, -1),
    )
    vmem = pl.BlockSpec(memory_space=pltpu.VMEM)
    result = pl.pallas_call(
        functools.partial(kernel, sky),
        out_shape=pltpu.VMEM((owned_rows + 8, win_cols), F32),
        in_specs=[pl.BlockSpec(memory_space=pl.ANY)] * 9,
        out_specs=vmem,
        scratch_shapes=[
            *[pltpu.VMEM(value.shape, value.dtype) for value in inputs],
            pltpu.VMEM((win_rows + 72, win_cols), F32),
            pltpu.VMEM((2, win_rows // 2 + 32, LANES), F32),
            pltpu.VMEM((2, win_rows // 2 + 32, LANES), F32),
            pltpu.VMEM((2, win_rows // 2 + 16, LANES), F32),
            pltpu.VMEM((2, (row_taps.shape[1] + 2) * win_cols // 2, LANES), BF16),
            pltpu.VMEM((2, (row_taps.shape[1] + 2) * 16, LANES), BF16),
            pltpu.VMEM((sky * (span // 2 + 2 * TILE_R), tiles * TILE_R // 2), BF16),
            pltpu.VMEM((2, 32, LANES), F32),
            pltpu.VMEM((row_taps.shape[1], 32, LANES), F32),
            pltpu.VMEM((2, win_rows // 2, 2 * LANES), F32),
            pltpu.VMEM((2, win_rows // 2 + 16, win_cols), F32),
            pltpu.VMEM((sky, span + 2 * TILE_R, win_cols), BF16),
            pltpu.VMEM((sky, span + 2 * TILE_R, win_cols), BF16),
            pltpu.SemaphoreType.DMA((9,)),
            pltpu.SemaphoreType.DMA,
            pltpu.SemaphoreType.DMA,
        ],
        compiler_params=pltpu.CompilerParams(collective_id=0, has_side_effects=True),
        name="coadd",
    )(*inputs)
    coadd, weight_map = pl.pallas_call(
        hand_over,
        out_shape=(
            jax.ShapeDtypeStruct((owned_rows, win_cols), F32),
            jax.ShapeDtypeStruct((1, owned_rows), F32),
        ),
        in_specs=[vmem],
        out_specs=(vmem, vmem),
        name="hand_over",
    )(pltpu.with_memory_space_constraint(result, pltpu.VMEM))
    return coadd, weight_map.reshape(owned_rows)


def solution(mesh):
    return jax.shard_map(
        on_device,
        mesh=mesh,
        in_specs=(
            P(("groups", "sky"), None, None),
            P(),
            P(),
            P(("groups", "sky"), None, None),
            P(("groups", "sky"), None),
            P(("groups", "sky")),
            P("groups"),
            P(("groups", "sky")),
            P(("groups", "sky")),
        ),
        out_specs=(P(("groups", "sky"), None), P(("groups", "sky"))),
        check_vma=False,
    )
```

```python
import functools

import jax
import jax.numpy as jnp
from jax import lax
from jax.experimental import pallas as pl
from jax.experimental.pallas import tpu as pltpu
from jax.sharding import PartitionSpec as P

TILE_R = 8
BLK_DEV = 16
LANES = 128
F32 = jnp.float32
BF16 = jnp.bfloat16


def iota(shape, axis):
    return lax.broadcasted_iota(jnp.int32, shape, axis)


def dot(lhs, rhs):
    return jnp.dot(lhs, rhs, preferred_element_type=F32)


def onehot(mask):
    return jnp.where(mask, 1.0, 0.0).astype(BF16)


def lanczos(fraction):
    lane = iota((1, LANES), 1)
    offsets = (lane - 2).astype(F32) - fraction
    offsets = jnp.where(lane < 6, offsets, 0.5)
    angles = jnp.pi * offsets
    thirds = angles / 3.0
    kernel = jnp.sin(angles) / angles * (jnp.sin(thirds) / thirds)
    kernel = jnp.where(lane < 6, kernel, 0.0)
    return kernel / jnp.sum(kernel, axis=1, keepdims=True)


def kernel(
    sky,
    *refs,
):
    sources = refs[0:9]
    result_ref = refs[9]
    (
        image_ref,
        row_taps_ref,
        col_taps_ref,
        mix_ref,
        shift_ref,
        visit_ref,
        visit_weight_ref,
        block_ref,
        offset_ref,
    ) = held = refs[10:19]
    (
        xpad,
        pairs,
        edges,
        quads,
        pick,
        taps2d,
        seeds,
        acc,
        spread_pad,
        data_send,
        data_recv,
        load_sem,
        data_ssem,
        data_rsem,
    ) = refs[19:]
    loads = [
        pltpu.make_async_copy(source, target, load_sem.at[number])
        for number, (source, target) in enumerate(zip(sources, held))
    ]
    for number in (1, 2, 3, 0, 7, 8, 5, 6, 4):
        loads[number].start()
    me = lax.axis_index("sky")
    win_rows, win_cols = image_ref.shape
    tap_count, basis = row_taps_ref.shape
    half = tap_count // 2
    tiles = block_ref.shape[1]
    cap = max(2, tiles // sky)
    span = cap * TILE_R
    owned_rows = BLK_DEV * TILE_R
    blk_shift = BLK_DEV.bit_length() - 1

    per_group = LANES // span
    spill_group = min(LANES // TILE_R, sky)
    barrier = pltpu.get_barrier_semaphore()

    def greet(step, carry):
        pl.semaphore_signal(
            barrier,
            inc=1,
            device_id={"sky": lax.rem(me + step, sky)},
            device_id_type=pl.DeviceIdType.MESH,
        )
        return carry

    lax.fori_loop(1, sky, greet, 0)

    xpad[0:16, :] = jnp.zeros((16, win_cols), F32)
    xpad[win_rows + 16 :, :] = jnp.zeros((xpad.shape[0] - win_rows - 16, win_cols), F32)
    for number in (1, 2, 3):
        loads[number].wait()

    def message(turn):
        to = turn - 1 + lax.div(turn - 1 - me + sky, jnp.int32(sky))
        return pltpu.make_async_remote_copy(
            src_ref=data_send.at[to],
            dst_ref=data_recv.at[me],
            send_sem=data_ssem,
            recv_sem=data_rsem,
            device_id={"sky": to},
            device_id_type=pl.DeviceIdType.MESH,
        )

    def arrivals(count):
        return pltpu.make_async_remote_copy(
            src_ref=data_send.at[pl.ds(0, count)],
            dst_ref=data_recv.at[pl.ds(0, count)],
            send_sem=data_ssem,
            recv_sem=data_rsem,
            device_id={"sky": lax.rem(me + 1, sky)},
            device_id_type=pl.DeviceIdType.MESH,
        )

    tap = iota((tap_count, 2 * LANES), 0)
    spot = iota((tap_count, 2 * LANES), 1)
    place = jnp.where(spot < LANES, 0, LANES // 2)
    flip = onehot(
        lax.rem(spot, jnp.int32(LANES)) == lax.rem(half + place - tap + LANES, jnp.int32(LANES))
    )
    flipped = lax.dot_general(
        row_taps_ref[...], flip, (((0,), (0,)), ((), ())), preferred_element_type=F32
    ).astype(BF16)
    near, far = flipped[:, 0:LANES], flipped[:, LANES:]

    def mixed(term, taps):
        value = col_taps_ref[...].astype(F32) * mix_ref[term]
        high = value.astype(BF16)
        low = (value - high.astype(F32)).astype(BF16)
        return dot(high, taps) + dot(low, taps)

    taps2d[0, 0:tap_count, :] = mixed(0, near) + mixed(2, far)
    taps2d[1, 0:tap_count, :] = mixed(1, near)

    side = win_cols // 2
    edge = 16
    pair_rows = win_rows // 2
    shifts = (tap_count + 1) // 2
    eight = (TILE_R, LANES)
    group = (edge, LANES)
    lane_of = iota(group, 1)
    signed = lax.rem(lane_of + side, jnp.int32(LANES)) - side
    column_pos = (2.0 * signed.astype(F32) + 1.0) / win_cols - 1.0
    in_side = lax.rem(iota(group, 1), jnp.int32(side))
    inside = {
        first: onehot(jnp.abs(iota(group, 0) + first - in_side) <= half)
        for first in range(-edge, side + edge, edge)
        if first < half or first + edge + half > side
    }

    def slanted(tap):
        fixed, slope = (
            pltpu.roll(
                jnp.broadcast_to(taps2d[term, tap : tap + 1, :], group),
                0,
                1,
                stride=1,
                stride_axis=0,
            )
            for term in range(2)
        )
        seeds[tap, 0:edge, :] = fixed + column_pos * slope
        seeds[tap, edge : 2 * edge, :] = slope

    def toeplitz(tap):
        value = seeds[tap, 0:16, :]
        step = (2.0 * edge / win_cols) * seeds[tap, 16:32, :]
        for column in range(0, win_cols, edge):
            rounded = value.astype(BF16)
            for part in range(2):
                first = column - side * part
                if -edge * part <= first < side + edge * (1 - part):
                    rows = pltpu.roll(rounded, first % LANES, 1) if first else rounded
                    if first in inside:
                        rows = rows * inside[first]
                    (body if 0 <= first < side else rim)[part].append(rows)
            value = value + step

    for tap in range(tap_count):
        slanted(tap)

    body, rim = ([], []), ([], [])
    for tap in range(0):
        toeplitz(tap)
    for number in (4, 5, 6, 7, 8, 0):
        loads[number].wait()
    xpad[pl.ds(16, win_rows), :] = image_ref[...].astype(F32)
    held_rows = pairs.shape[1]
    lane_of = iota((held_rows, LANES), 1)
    low = onehot(lane_of < side)
    high = onehot(lane_of >= side)
    odd = xpad[pl.ds(1, held_rows, stride=2), :].astype(BF16)
    even = xpad[pl.ds(2, held_rows, stride=2), :].astype(BF16)
    west = odd * low + pltpu.roll(even, side, 1) * high
    east = pltpu.roll(odd, side, 1) * low + even * high
    pairs[0] = west.astype(F32)
    pairs[1] = east.astype(F32)

    for tap in range(0, tap_count):
        toeplitz(tap)

    block = block_ref[...]
    owner_i = lax.shift_right_logical(block, blk_shift)
    start_row = ((block - owner_i * BLK_DEV) * TILE_R + offset_ref[...]).astype(F32)
    owner_row = owner_i.astype(F32)
    eye = iota((tiles, tiles), 0) == iota((tiles, tiles), 1)
    column = lambda row: jnp.sum(
        jnp.where(eye, jnp.broadcast_to(row, (tiles, tiles)), 0.0), axis=1, keepdims=True
    )
    owner_col = column(owner_row)
    start_col = column(start_row)
    same = owner_col == owner_row
    below = iota((tiles, tiles), 0) < iota((tiles, tiles), 1)
    above = iota((tiles, tiles), 1) < iota((tiles, tiles), 0)
    rank_row = jnp.sum(jnp.where(same & below, 1.0, 0.0), axis=0, keepdims=True)
    rank_col = jnp.sum(jnp.where(same & above, 1.0, 0.0), axis=1, keepdims=True)
    visits = visit_weight_ref.shape[1]
    own_weight = jnp.sum(
        jnp.where(
            iota((1, visits), 1) == visit_ref[...], visit_weight_ref[...].astype(F32), 0.0
        ),
        axis=1,
        keepdims=True,
    )

    sub = iota((sky * TILE_R, tiles), 0)
    owner_of = lax.shift_right_logical(sub, 3).astype(F32)
    lane = iota((tiles, LANES), 1)
    mine = lax.div(lane, jnp.int32(span)) == lax.rem(me, per_group)
    local = lax.rem(lane, jnp.int32(span))
    parity = lax.div(local, jnp.int32(span // 2))
    local = lax.rem(local, jnp.int32(span // 2))
    slot_rank = lax.div(local, jnp.int32(TILE_R // 2)).astype(F32)
    in_eight = (2 * lax.rem(local, jnp.int32(TILE_R // 2)) + parity).astype(F32)
    landing = jnp.where(mine & (slot_rank == rank_col), start_col + in_eight + 1.0, 0.0)
    in_eight = lax.rem(lane, jnp.int32(TILE_R)).astype(F32)
    targets = dot(onehot(owner_of == owner_row), landing.astype(BF16))
    mine = lax.div(lane, jnp.int32(TILE_R)) == lax.rem(me, spill_group)
    cover = onehot(mine & (start_col > in_eight + float(owned_rows - TILE_R)))
    covered = dot(onehot(owner_of - 1.0 == owner_row), cover)
    lane8 = iota((sky * TILE_R, LANES), 1)
    sub8 = lax.rem(iota((sky * TILE_R, LANES), 0), jnp.int32(TILE_R))
    weight8 = jnp.broadcast_to(own_weight, (sky * TILE_R, LANES))
    tile_lanes = lax.div(lane8, jnp.int32(span)) == lax.rem(me, per_group)
    spill_lanes = lax.div(lane8, jnp.int32(TILE_R)) == lax.rem(me, spill_group)
    header = jnp.where((sub8 == 1) & tile_lanes, weight8, 0.0)
    header = jnp.where((sub8 == 2) & spill_lanes, weight8, header)
    header = jnp.where(sub8 == 3, covered, header)
    header = jnp.where(sub8 == 0, targets, header)
    data_send[:, span + TILE_R :, :] = header.reshape(sky, TILE_R, LANES).astype(BF16)

    wide = tiles * TILE_R // 2
    widen = onehot(
        iota((tiles, wide), 0) == lax.shift_right_logical(iota((tiles, wide), 1), 2)
    )
    in_tile = (2 * lax.rem(iota((1, wide), 1), jnp.int32(TILE_R // 2))).astype(F32)
    spread8 = lambda row: dot(jnp.broadcast_to(row, (8, tiles)).astype(BF16), widen)[0:1, :]
    owner_wide = spread8(owner_row)
    slot_lane = spread8(owner_row * cap + rank_row) * (TILE_R // 2) + in_tile / 2.0
    cuts = (0, sky // 4, sky // 2, sky)
    pick_rows = span // 2 + 2 * TILE_R
    past = spread8(start_row) + in_tile - float(owned_rows)
    spill_lanes = []
    for parity in range(2):
        moved = past + float(parity)
        spill_lanes.append(jnp.where(moved >= 0.0, (owner_wide + 1.0) * TILE_R + moved, -1.0))
    for first, last in zip(cuts, cuts[1:]):
        base = first * pick_rows
        for rows, lanes in ((span // 2, slot_lane), (TILE_R, spill_lanes[0]), (TILE_R, spill_lanes[1])):
            count = (last - first) * rows
            place = (iota((count, wide), 0) + first * rows).astype(F32)
            pick[base : base + count, :] = onehot(place == lanes)
            base += count

    low = onehot(lane_of < edge)
    high = onehot((lane_of >= edge) & (lane_of < 2 * edge))
    quad_rows = quads.shape[1]
    quarter = lax.div(iota((quad_rows, LANES), 1), jnp.int32(2 * edge))
    for part in range(2):
        if part:
            strip = pltpu.roll(west, edge + side, 1) * low + pltpu.roll(west, 2 * edge, 1) * high
        else:
            strip = east * low + pltpu.roll(east, edge + side, 1) * high
        strip = strip + pltpu.roll(strip, 2 * edge, 1)
        strip = strip + pltpu.roll(strip, 4 * edge, 1)
        edges[part] = strip.astype(F32)
        value = edges[part, 0:quad_rows, :]
        for later in range(1, 4):
            value = jnp.where(quarter == later, edges[part, pl.ds(later, quad_rows), :], value)
        quads[part] = value

    def product(part):
        left = [pairs[part, pl.ds(shift, pair_rows), :].astype(BF16) for shift in range(shifts)]
        left += [
            quads[part, pl.ds(first, pair_rows), :].astype(BF16) for first in range(0, shifts, 4)
        ]
        gap = jnp.zeros(group, BF16)
        gaps = [gap] * (side // edge)
        early = jnp.concatenate([*body[part], *gaps, *rim[part], gap], axis=0)
        late = jnp.concatenate([*gaps, *body[part], gap, *rim[part]], axis=0)
        return dot(jnp.concatenate(left, axis=1), jnp.concatenate([early, late], axis=1))

    for part in range(2):
        acc[part] = product(part)

    across = lanczos(shift_ref[0:1, 1:2])
    down = lanczos(shift_ref[0:1, 0:1])
    chunk = min(64, pair_rows)
    for parity in range(2):
        spread_pad[parity, 0:8, :] = jnp.zeros((8, win_cols), F32)
        spread_pad[parity, pair_rows + 8 :, :] = jnp.zeros((8, win_cols), F32)
    down_taps = [
        jnp.broadcast_to(down[0:1, m + 2 : m + 3], (1, win_cols)) for m in range(-2, 4)
    ]
    square = (2 * LANES, LANES)
    pixel = lax.div(iota(square, 0), jnp.int32(LANES)) * side + lax.rem(
        iota(square, 0), jnp.int32(side)
    )
    warp = jnp.zeros(square, F32)
    for m in range(-2, 4):
        warp = jnp.where(pixel - iota(square, 1) == m, across[0:1, m + 2 : m + 3], warp)
    warp_high = warp.astype(BF16)
    warp_low = (warp - warp_high.astype(F32)).astype(BF16)
    warp_both = jnp.concatenate([warp_high, warp_low], axis=1)
    in_first = iota((chunk, LANES), 1) < side
    for first in range(0, pair_rows, chunk):
        here = slice(first, first + chunk)
        for parity in range(2):
            columns = slice(parity * LANES, (parity + 1) * LANES)
            row_pos = (2 * (iota((chunk, LANES), 0) + first) + parity).astype(F32)
            row_pos = (2.0 * row_pos + 1.0) / win_rows - 1.0
            factor = jnp.where(in_first, 1.0, row_pos)
            terms = jnp.concatenate(
                [acc[0, here, columns] * factor, acc[1, here, columns] * factor], axis=1
            )
            high = terms.astype(BF16)
            low = (terms - high.astype(F32)).astype(BF16)
            both = dot(high, warp_both)
            spread = both[:, 0:LANES] + both[:, LANES:] + dot(low, warp_high)
            spread_pad[parity, first + 8 : first + 8 + chunk, :] = spread
    warped = []
    for parity in range(2):
        rows = []
        for first in range(0, pair_rows, chunk):
            value = None
            for m in range(-2, 4):
                other = (parity + m) % 2
                down_by = (parity + m - other) // 2
                term = down_taps[m + 2] * spread_pad[other, pl.ds(first + 8 + down_by, chunk), :]
                value = term if value is None else value + term
            rows.append(value.astype(BF16))
        warped.append(jnp.concatenate(rows, axis=0))
    warped = jnp.concatenate(warped, axis=1)

    pl.semaphore_wait(barrier, sky - 1)
    for first, last in zip(cuts, cuts[1:]):
        packed = dot(pick[first * pick_rows : last * pick_rows, :], warped)
        count = last - first
        sent, spills = count * span // 2, count * TILE_R
        halves = [
            packed[0:sent, parity * LANES : (parity + 1) * LANES].reshape(count, span // 2, win_cols)
            for parity in range(2)
        ]
        data_send[first:last, 0:span, :] = jnp.concatenate(halves, axis=1).astype(BF16)
        spilled = packed[sent : sent + spills, 0:LANES] + packed[sent + spills :, LANES:]
        data_send[first:last, span : span + TILE_R, :] = spilled.reshape(
            count, TILE_R, win_cols
        ).astype(BF16)

        def start_data(step, carry):
            message(step).start()
            return carry

        lax.fori_loop(max(first, 1), last, start_data, 0)
    data_recv[pl.ds(me, 1)] = data_send[pl.ds(me, 1)]

    arrivals(sky - 1).wait_recv()

    owned = (owned_rows, LANES)
    row_id = (iota(owned, 0) + 1).astype(F32)
    places = []
    total = jnp.zeros((owned_rows, win_cols), F32)
    ones = jnp.ones((LANES, win_cols), BF16)
    for group in range(sky // per_group):
        head = data_recv[group * per_group : (group + 1) * per_group, span + TILE_R :, :]
        head = jnp.sum(head.astype(F32), axis=0)
        place = jnp.where(head[0:1, :] == row_id, head[1:2, :], 0.0).astype(BF16)
        places.append(place)
        total = total + dot(place, ones)
    spill_places = []
    same_row = lax.rem(iota(owned, 1), jnp.int32(TILE_R)) == iota(owned, 0)
    here_row = lax.rem(iota(eight, 1), jnp.int32(TILE_R)) == iota(eight, 0)
    first_rows = jnp.zeros(eight, F32)
    for group in range(sky // spill_group):
        head = data_recv[group * spill_group : (group + 1) * spill_group, span + TILE_R :, :]
        head = jnp.sum(head.astype(F32), axis=0)
        spill_places.append(jnp.where(same_row, head[2:3, :], 0.0).astype(BF16))
        count = jnp.sum(jnp.where(here_row, head[2:3, :] * head[3:4, :], 0.0), axis=1, keepdims=True)
        first_rows = first_rows + jnp.broadcast_to(count, eight)
    total = total + jnp.concatenate(
        [first_rows, jnp.zeros((owned_rows - TILE_R, LANES), F32)], axis=0
    )
    diagonal = iota(owned, 0) == iota(owned, 1)
    result_ref[owned_rows:, :] = jnp.broadcast_to(
        jnp.sum(jnp.where(diagonal, total, 0.0), axis=0, keepdims=True), (8, LANES)
    )

    sums = jnp.zeros((owned_rows, win_cols), F32)
    for group, place in enumerate(places):
        part = data_recv[group * per_group : (group + 1) * per_group, 0:span, :]
        sums = sums + dot(place, part.reshape(LANES, win_cols))
    for group, place in enumerate(spill_places):
        part = data_recv[group * spill_group : (group + 1) * spill_group, span : span + TILE_R, :]
        part = part.astype(F32).reshape(spill_group * TILE_R, win_cols).astype(BF16)
        sums = sums + dot(place[:, 0 : spill_group * TILE_R], part)
    result_ref[0:owned_rows, :] = sums / jnp.maximum(total, 1.0)
    arrivals(sky - 1).wait_send()


def hand_over(result_ref, coadd_ref, weight_ref):
    owned_rows = coadd_ref.shape[0]
    coadd_ref[...] = result_ref[0:owned_rows, :]
    weight_ref[...] = result_ref[owned_rows : owned_rows + 1, :]


def on_device(
    image,
    row_taps,
    col_taps,
    mix_coeff,
    shift_frac,
    ccd_visit,
    visit_weight,
    tile_block,
    tile_offset,
):
    sky = lax.axis_size("sky")
    win_rows, win_cols = image.shape[1:]
    tiles = tile_block.shape[0]
    span = max(2, tiles // sky) * TILE_R
    owned_rows = BLK_DEV * TILE_R
    inputs = (
        image[0],
        row_taps.T,
        col_taps.T,
        mix_coeff.transpose(1, 0, 2),
        shift_frac,
        ccd_visit.reshape(1, 1),
        visit_weight.reshape(1, -1),
        tile_block.reshape(1, -1),
        tile_offset.reshape(1, -1),
    )
    vmem = pl.BlockSpec(memory_space=pltpu.VMEM)
    result = pl.pallas_call(
        functools.partial(kernel, sky),
        out_shape=pltpu.VMEM((owned_rows + 8, win_cols), F32),
        in_specs=[pl.BlockSpec(memory_space=pl.ANY)] * 9,
        out_specs=vmem,
        scratch_shapes=[
            *[pltpu.VMEM(value.shape, value.dtype) for value in inputs],
            pltpu.VMEM((win_rows + 72, win_cols), F32),
            pltpu.VMEM((2, win_rows // 2 + 32, LANES), F32),
            pltpu.VMEM((2, win_rows // 2 + 32, LANES), F32),
            pltpu.VMEM((2, win_rows // 2 + 16, LANES), F32),
            pltpu.VMEM((sky * (span // 2 + 2 * TILE_R), tiles * TILE_R // 2), BF16),
            pltpu.VMEM((2, 32, LANES), F32),
            pltpu.VMEM((row_taps.shape[1], 32, LANES), F32),
            pltpu.VMEM((2, win_rows // 2, 2 * LANES), F32),
            pltpu.VMEM((2, win_rows // 2 + 16, win_cols), F32),
            pltpu.VMEM((sky, span + 2 * TILE_R, win_cols), BF16),
            pltpu.VMEM((sky, span + 2 * TILE_R, win_cols), BF16),
            pltpu.SemaphoreType.DMA((9,)),
            pltpu.SemaphoreType.DMA,
            pltpu.SemaphoreType.DMA,
        ],
        compiler_params=pltpu.CompilerParams(collective_id=0, has_side_effects=True),
        name="coadd",
    )(*inputs)
    coadd, weight_map = pl.pallas_call(
        hand_over,
        out_shape=(
            jax.ShapeDtypeStruct((owned_rows, win_cols), F32),
            jax.ShapeDtypeStruct((1, owned_rows), F32),
        ),
        in_specs=[vmem],
        out_specs=(vmem, vmem),
        name="hand_over",
    )(pltpu.with_memory_space_constraint(result, pltpu.VMEM))
    return coadd, weight_map.reshape(owned_rows)


def solution(mesh):
    return jax.shard_map(
        on_device,
        mesh=mesh,
        in_specs=(
            P(("groups", "sky"), None, None),
            P(),
            P(),
            P(("groups", "sky"), None, None),
            P(("groups", "sky"), None),
            P(("groups", "sky")),
            P("groups"),
            P(("groups", "sky")),
            P(("groups", "sky")),
        ),
        out_specs=(P(("groups", "sky"), None), P(("groups", "sky"))),
        check_vma=False,
    )
```

```python
import functools

import jax
import jax.numpy as jnp
from jax import lax
from jax.experimental import pallas as pl
from jax.experimental.pallas import tpu as pltpu
from jax.sharding import PartitionSpec as P

TILE_R = 8
BLK_DEV = 16
LANES = 128
F32 = jnp.float32
BF16 = jnp.bfloat16


def iota(shape, axis):
    return lax.broadcasted_iota(jnp.int32, shape, axis)


def dot(lhs, rhs):
    return jnp.dot(lhs, rhs, preferred_element_type=F32)


def onehot(mask):
    return jnp.where(mask, 1.0, 0.0).astype(BF16)


def lanczos(fraction):
    lane = iota((1, LANES), 1)
    offsets = (lane - 2).astype(F32) - fraction
    offsets = jnp.where(lane < 6, offsets, 0.5)
    angles = jnp.pi * offsets
    thirds = angles / 3.0
    kernel = jnp.sin(angles) / angles * (jnp.sin(thirds) / thirds)
    kernel = jnp.where(lane < 6, kernel, 0.0)
    return kernel / jnp.sum(kernel, axis=1, keepdims=True)


def kernel(
    sky,
    *refs,
):
    sources = refs[0:9]
    result_ref = refs[9]
    (
        image_ref,
        row_taps_ref,
        col_taps_ref,
        mix_ref,
        shift_ref,
        visit_ref,
        visit_weight_ref,
        block_ref,
        offset_ref,
    ) = held = refs[10:19]
    (
        xpad,
        pairs,
        edges,
        quads,
        pick,
        taps2d,
        seeds,
        acc,
        spread_pad,
        data_send,
        data_recv,
        load_sem,
        data_ssem,
        data_rsem,
    ) = refs[19:]
    loads = [
        pltpu.make_async_copy(source, target, load_sem.at[number])
        for number, (source, target) in enumerate(zip(sources, held))
    ]
    for number in (1, 2, 3, 0, 7, 8, 5, 6, 4):
        loads[number].start()
    me = lax.axis_index("sky")
    win_rows, win_cols = image_ref.shape
    tap_count, basis = row_taps_ref.shape
    half = tap_count // 2
    tiles = block_ref.shape[1]
    cap = max(2, tiles // sky)
    span = cap * TILE_R
    owned_rows = BLK_DEV * TILE_R
    blk_shift = BLK_DEV.bit_length() - 1

    per_group = LANES // span
    spill_group = min(LANES // TILE_R, sky)
    barrier = pltpu.get_barrier_semaphore()

    def greet(step, carry):
        pl.semaphore_signal(
            barrier,
            inc=1,
            device_id={"sky": lax.rem(me + step, sky)},
            device_id_type=pl.DeviceIdType.MESH,
        )
        return carry

    lax.fori_loop(1, sky, greet, 0)

    xpad[0:16, :] = jnp.zeros((16, win_cols), F32)
    xpad[win_rows + 16 :, :] = jnp.zeros((xpad.shape[0] - win_rows - 16, win_cols), F32)
    for number in (1, 2, 3, 5, 6, 7, 8):
        loads[number].wait()

    def message(turn):
        to = turn - 1 + lax.div(turn - 1 - me + sky, jnp.int32(sky))
        return pltpu.make_async_remote_copy(
            src_ref=data_send.at[to],
            dst_ref=data_recv.at[me],
            send_sem=data_ssem,
            recv_sem=data_rsem,
            device_id={"sky": to},
            device_id_type=pl.DeviceIdType.MESH,
        )

    def arrivals(count):
        return pltpu.make_async_remote_copy(
            src_ref=data_send.at[pl.ds(0, count)],
            dst_ref=data_recv.at[pl.ds(0, count)],
            send_sem=data_ssem,
            recv_sem=data_rsem,
            device_id={"sky": lax.rem(me + 1, sky)},
            device_id_type=pl.DeviceIdType.MESH,
        )

    tap = iota((tap_count, 2 * LANES), 0)
    spot = iota((tap_count, 2 * LANES), 1)
    place = jnp.where(spot < LANES, 0, LANES // 2)
    flip = onehot(
        lax.rem(spot, jnp.int32(LANES)) == lax.rem(half + place - tap + LANES, jnp.int32(LANES))
    )
    flipped = lax.dot_general(
        row_taps_ref[...], flip, (((0,), (0,)), ((), ())), preferred_element_type=F32
    ).astype(BF16)
    near, far = flipped[:, 0:LANES], flipped[:, LANES:]

    def mixed(term, taps):
        value = col_taps_ref[...].astype(F32) * mix_ref[term]
        high = value.astype(BF16)
        low = (value - high.astype(F32)).astype(BF16)
        return dot(high, taps) + dot(low, taps)

    taps2d[0, 0:tap_count, :] = mixed(0, near) + mixed(2, far)
    taps2d[1, 0:tap_count, :] = mixed(1, near)

    side = win_cols // 2
    edge = 16
    pair_rows = win_rows // 2
    shifts = (tap_count + 1) // 2
    eight = (TILE_R, LANES)
    group = (edge, LANES)
    lane_of = iota(group, 1)
    signed = lax.rem(lane_of + side, jnp.int32(LANES)) - side
    column_pos = (2.0 * signed.astype(F32) + 1.0) / win_cols - 1.0
    in_side = lax.rem(iota(group, 1), jnp.int32(side))
    inside = {
        first: onehot(jnp.abs(iota(group, 0) + first - in_side) <= half)
        for first in range(-edge, side + edge, edge)
        if first < half or first + edge + half > side
    }

    def slanted(tap):
        fixed, slope = (
            pltpu.roll(
                jnp.broadcast_to(taps2d[term, tap : tap + 1, :], group),
                0,
                1,
                stride=1,
                stride_axis=0,
            )
            for term in range(2)
        )
        seeds[tap, 0:edge, :] = fixed + column_pos * slope
        seeds[tap, edge : 2 * edge, :] = slope

    def toeplitz(tap):
        value = seeds[tap, 0:16, :]
        step = (2.0 * edge / win_cols) * seeds[tap, 16:32, :]
        for column in range(0, win_cols, edge):
            rounded = value.astype(BF16)
            for part in range(2):
                first = column - side * part
                if -edge * part <= first < side + edge * (1 - part):
                    rows = pltpu.roll(rounded, first % LANES, 1) if first else rounded
                    if first in inside:
                        rows = rows * inside[first]
                    (body if 0 <= first < side else rim)[part].append(rows)
            value = value + step


    body, rim = ([], []), ([], [])
    block = block_ref[...]
    owner_i = lax.shift_right_logical(block, blk_shift)
    start_row = ((block - owner_i * BLK_DEV) * TILE_R + offset_ref[...]).astype(F32)
    owner_row = owner_i.astype(F32)
    eye = iota((tiles, tiles), 0) == iota((tiles, tiles), 1)
    column = lambda row: jnp.sum(
        jnp.where(eye, jnp.broadcast_to(row, (tiles, tiles)), 0.0), axis=1, keepdims=True
    )
    owner_col = column(owner_row)
    start_col = column(start_row)
    same = owner_col == owner_row
    below = iota((tiles, tiles), 0) < iota((tiles, tiles), 1)
    above = iota((tiles, tiles), 1) < iota((tiles, tiles), 0)
    rank_row = jnp.sum(jnp.where(same & below, 1.0, 0.0), axis=0, keepdims=True)
    rank_col = jnp.sum(jnp.where(same & above, 1.0, 0.0), axis=1, keepdims=True)
    visits = visit_weight_ref.shape[1]
    own_weight = jnp.sum(
        jnp.where(
            iota((1, visits), 1) == visit_ref[...], visit_weight_ref[...].astype(F32), 0.0
        ),
        axis=1,
        keepdims=True,
    )

    sub = iota((sky * TILE_R, tiles), 0)
    owner_of = lax.shift_right_logical(sub, 3).astype(F32)
    lane = iota((tiles, LANES), 1)
    mine = lax.div(lane, jnp.int32(span)) == lax.rem(me, per_group)
    local = lax.rem(lane, jnp.int32(span))
    parity = lax.div(local, jnp.int32(span // 2))
    local = lax.rem(local, jnp.int32(span // 2))
    slot_rank = lax.div(local, jnp.int32(TILE_R // 2)).astype(F32)
    in_eight = (2 * lax.rem(local, jnp.int32(TILE_R // 2)) + parity).astype(F32)
    landing = jnp.where(mine & (slot_rank == rank_col), start_col + in_eight + 1.0, 0.0)
    in_eight = lax.rem(lane, jnp.int32(TILE_R)).astype(F32)
    targets = dot(onehot(owner_of == owner_row), landing.astype(BF16))
    mine = lax.div(lane, jnp.int32(TILE_R)) == lax.rem(me, spill_group)
    cover = onehot(mine & (start_col > in_eight + float(owned_rows - TILE_R)))
    covered = dot(onehot(owner_of - 1.0 == owner_row), cover)
    lane8 = iota((sky * TILE_R, LANES), 1)
    sub8 = lax.rem(iota((sky * TILE_R, LANES), 0), jnp.int32(TILE_R))
    weight8 = jnp.broadcast_to(own_weight, (sky * TILE_R, LANES))
    tile_lanes = lax.div(lane8, jnp.int32(span)) == lax.rem(me, per_group)
    spill_lanes = lax.div(lane8, jnp.int32(TILE_R)) == lax.rem(me, spill_group)
    header = jnp.where((sub8 == 1) & tile_lanes, weight8, 0.0)
    header = jnp.where((sub8 == 2) & spill_lanes, weight8, header)
    header = jnp.where(sub8 == 3, covered, header)
    header = jnp.where(sub8 == 0, targets, header)
    data_send[:, span + TILE_R :, :] = header.reshape(sky, TILE_R, LANES).astype(BF16)

    wide = tiles * TILE_R // 2
    widen = onehot(
        iota((tiles, wide), 0) == lax.shift_right_logical(iota((tiles, wide), 1), 2)
    )
    in_tile = (2 * lax.rem(iota((1, wide), 1), jnp.int32(TILE_R // 2))).astype(F32)
    spread8 = lambda row: dot(jnp.broadcast_to(row, (8, tiles)).astype(BF16), widen)[0:1, :]
    owner_wide = spread8(owner_row)
    slot_lane = spread8(owner_row * cap + rank_row) * (TILE_R // 2) + in_tile / 2.0
    cuts = (0, sky // 4, sky // 2, sky)
    pick_rows = span // 2 + 2 * TILE_R
    past = spread8(start_row) + in_tile - float(owned_rows)
    spill_lanes = []
    for parity in range(2):
        moved = past + float(parity)
        spill_lanes.append(jnp.where(moved >= 0.0, (owner_wide + 1.0) * TILE_R + moved, -1.0))
    for first, last in zip(cuts, cuts[1:]):
        base = first * pick_rows
        for rows, lanes in ((span // 2, slot_lane), (TILE_R, spill_lanes[0]), (TILE_R, spill_lanes[1])):
            count = (last - first) * rows
            place = (iota((count, wide), 0) + first * rows).astype(F32)
            pick[base : base + count, :] = onehot(place == lanes)
            base += count

    loads[4].wait()
    for tap in range(tap_count):
        slanted(tap)
    loads[0].wait()
    xpad[pl.ds(16, win_rows), :] = image_ref[...].astype(F32)
    held_rows = pairs.shape[1]
    lane_of = iota((held_rows, LANES), 1)
    low = onehot(lane_of < side)
    high = onehot(lane_of >= side)
    odd = xpad[pl.ds(1, held_rows, stride=2), :].astype(BF16)
    even = xpad[pl.ds(2, held_rows, stride=2), :].astype(BF16)
    west = odd * low + pltpu.roll(even, side, 1) * high
    east = pltpu.roll(odd, side, 1) * low + even * high
    pairs[0] = west.astype(F32)
    pairs[1] = east.astype(F32)

    for tap in range(0, tap_count):
        toeplitz(tap)

    low = onehot(lane_of < edge)
    high = onehot((lane_of >= edge) & (lane_of < 2 * edge))
    quad_rows = quads.shape[1]
    quarter = lax.div(iota((quad_rows, LANES), 1), jnp.int32(2 * edge))
    for part in range(2):
        if part:
            strip = pltpu.roll(west, edge + side, 1) * low + pltpu.roll(west, 2 * edge, 1) * high
        else:
            strip = east * low + pltpu.roll(east, edge + side, 1) * high
        strip = strip + pltpu.roll(strip, 2 * edge, 1)
        strip = strip + pltpu.roll(strip, 4 * edge, 1)
        edges[part] = strip.astype(F32)
        value = edges[part, 0:quad_rows, :]
        for later in range(1, 4):
            value = jnp.where(quarter == later, edges[part, pl.ds(later, quad_rows), :], value)
        quads[part] = value

    def product(part):
        left = [pairs[part, pl.ds(shift, pair_rows), :].astype(BF16) for shift in range(shifts)]
        left += [
            quads[part, pl.ds(first, pair_rows), :].astype(BF16) for first in range(0, shifts, 4)
        ]
        gap = jnp.zeros(group, BF16)
        gaps = [gap] * (side // edge)
        early = jnp.concatenate([*body[part], *gaps, *rim[part], gap], axis=0)
        late = jnp.concatenate([*gaps, *body[part], gap, *rim[part]], axis=0)
        return dot(jnp.concatenate(left, axis=1), jnp.concatenate([early, late], axis=1))

    for part in range(2):
        acc[part] = product(part)

    across = lanczos(shift_ref[0:1, 1:2])
    down = lanczos(shift_ref[0:1, 0:1])
    chunk = min(256, pair_rows)
    for parity in range(2):
        spread_pad[parity, 0:8, :] = jnp.zeros((8, win_cols), F32)
        spread_pad[parity, pair_rows + 8 :, :] = jnp.zeros((8, win_cols), F32)
    down_taps = [
        jnp.broadcast_to(down[0:1, m + 2 : m + 3], (1, win_cols)) for m in range(-2, 4)
    ]
    square = (2 * LANES, LANES)
    pixel = lax.div(iota(square, 0), jnp.int32(LANES)) * side + lax.rem(
        iota(square, 0), jnp.int32(side)
    )
    warp = jnp.zeros(square, F32)
    for m in range(-2, 4):
        warp = jnp.where(pixel - iota(square, 1) == m, across[0:1, m + 2 : m + 3], warp)
    warp_high = warp.astype(BF16)
    warp_low = (warp - warp_high.astype(F32)).astype(BF16)
    warp_both = jnp.concatenate([warp_high, warp_low], axis=1)
    in_first = iota((chunk, LANES), 1) < side
    for first in range(0, pair_rows, chunk):
        here = slice(first, first + chunk)
        for parity in range(2):
            columns = slice(parity * LANES, (parity + 1) * LANES)
            row_pos = (2 * (iota((chunk, LANES), 0) + first) + parity).astype(F32)
            row_pos = (2.0 * row_pos + 1.0) / win_rows - 1.0
            factor = jnp.where(in_first, 1.0, row_pos)
            terms = jnp.concatenate(
                [acc[0, here, columns] * factor, acc[1, here, columns] * factor], axis=1
            )
            high = terms.astype(BF16)
            low = (terms - high.astype(F32)).astype(BF16)
            both = dot(high, warp_both)
            spread = both[:, 0:LANES] + both[:, LANES:] + dot(low, warp_high)
            spread_pad[parity, first + 8 : first + 8 + chunk, :] = spread
    warped = []
    for parity in range(2):
        rows = []
        for first in range(0, pair_rows, chunk):
            value = None
            for m in range(-2, 4):
                other = (parity + m) % 2
                down_by = (parity + m - other) // 2
                term = down_taps[m + 2] * spread_pad[other, pl.ds(first + 8 + down_by, chunk), :]
                value = term if value is None else value + term
            rows.append(value.astype(BF16))
        warped.append(jnp.concatenate(rows, axis=0))
    warped = jnp.concatenate(warped, axis=1)

    pl.semaphore_wait(barrier, sky - 1)
    for first, last in zip(cuts, cuts[1:]):
        packed = dot(pick[first * pick_rows : last * pick_rows, :], warped)
        count = last - first
        sent, spills = count * span // 2, count * TILE_R
        halves = [
            packed[0:sent, parity * LANES : (parity + 1) * LANES].reshape(count, span // 2, win_cols)
            for parity in range(2)
        ]
        data_send[first:last, 0:span, :] = jnp.concatenate(halves, axis=1).astype(BF16)
        spilled = packed[sent : sent + spills, 0:LANES] + packed[sent + spills :, LANES:]
        data_send[first:last, span : span + TILE_R, :] = spilled.reshape(
            count, TILE_R, win_cols
        ).astype(BF16)

        def start_data(step, carry):
            message(step).start()
            return carry

        lax.fori_loop(max(first, 1), last, start_data, 0)
    data_recv[pl.ds(me, 1)] = data_send[pl.ds(me, 1)]

    arrivals(sky - 1).wait_recv()

    owned = (owned_rows, LANES)
    row_id = (iota(owned, 0) + 1).astype(F32)
    places = []
    total = jnp.zeros((owned_rows, win_cols), F32)
    ones = jnp.ones((LANES, win_cols), BF16)
    for group in range(sky // per_group):
        head = data_recv[group * per_group : (group + 1) * per_group, span + TILE_R :, :]
        head = jnp.sum(head.astype(F32), axis=0)
        place = jnp.where(head[0:1, :] == row_id, head[1:2, :], 0.0).astype(BF16)
        places.append(place)
        total = total + dot(place, ones)
    spill_places = []
    same_row = lax.rem(iota(owned, 1), jnp.int32(TILE_R)) == iota(owned, 0)
    here_row = lax.rem(iota(eight, 1), jnp.int32(TILE_R)) == iota(eight, 0)
    first_rows = jnp.zeros(eight, F32)
    for group in range(sky // spill_group):
        head = data_recv[group * spill_group : (group + 1) * spill_group, span + TILE_R :, :]
        head = jnp.sum(head.astype(F32), axis=0)
        spill_places.append(jnp.where(same_row, head[2:3, :], 0.0).astype(BF16))
        count = jnp.sum(jnp.where(here_row, head[2:3, :] * head[3:4, :], 0.0), axis=1, keepdims=True)
        first_rows = first_rows + jnp.broadcast_to(count, eight)
    total = total + jnp.concatenate(
        [first_rows, jnp.zeros((owned_rows - TILE_R, LANES), F32)], axis=0
    )
    diagonal = iota(owned, 0) == iota(owned, 1)
    result_ref[owned_rows:, :] = jnp.broadcast_to(
        jnp.sum(jnp.where(diagonal, total, 0.0), axis=0, keepdims=True), (8, LANES)
    )

    sums = jnp.zeros((owned_rows, win_cols), F32)
    for group, place in enumerate(places):
        part = data_recv[group * per_group : (group + 1) * per_group, 0:span, :]
        sums = sums + dot(place, part.reshape(LANES, win_cols))
    for group, place in enumerate(spill_places):
        part = data_recv[group * spill_group : (group + 1) * spill_group, span : span + TILE_R, :]
        part = part.astype(F32).reshape(spill_group * TILE_R, win_cols).astype(BF16)
        sums = sums + dot(place[:, 0 : spill_group * TILE_R], part)
    result_ref[0:owned_rows, :] = sums / jnp.maximum(total, 1.0)
    arrivals(sky - 1).wait_send()


def hand_over(result_ref, coadd_ref, weight_ref):
    owned_rows = coadd_ref.shape[0]
    coadd_ref[...] = result_ref[0:owned_rows, :]
    weight_ref[...] = result_ref[owned_rows : owned_rows + 1, :]


def on_device(
    image,
    row_taps,
    col_taps,
    mix_coeff,
    shift_frac,
    ccd_visit,
    visit_weight,
    tile_block,
    tile_offset,
):
    sky = lax.axis_size("sky")
    win_rows, win_cols = image.shape[1:]
    tiles = tile_block.shape[0]
    span = max(2, tiles // sky) * TILE_R
    owned_rows = BLK_DEV * TILE_R
    inputs = (
        image[0],
        row_taps.T,
        col_taps.T,
        mix_coeff.transpose(1, 0, 2),
        shift_frac,
        ccd_visit.reshape(1, 1),
        visit_weight.reshape(1, -1),
        tile_block.reshape(1, -1),
        tile_offset.reshape(1, -1),
    )
    vmem = pl.BlockSpec(memory_space=pltpu.VMEM)
    result = pl.pallas_call(
        functools.partial(kernel, sky),
        out_shape=pltpu.VMEM((owned_rows + 8, win_cols), F32),
        in_specs=[pl.BlockSpec(memory_space=pl.ANY)] * 9,
        out_specs=vmem,
        scratch_shapes=[
            *[pltpu.VMEM(value.shape, value.dtype) for value in inputs],
            pltpu.VMEM((win_rows + 72, win_cols), F32),
            pltpu.VMEM((2, win_rows // 2 + 32, LANES), F32),
            pltpu.VMEM((2, win_rows // 2 + 32, LANES), F32),
            pltpu.VMEM((2, win_rows // 2 + 16, LANES), F32),
            pltpu.VMEM((sky * (span // 2 + 2 * TILE_R), tiles * TILE_R // 2), BF16),
            pltpu.VMEM((2, 32, LANES), F32),
            pltpu.VMEM((row_taps.shape[1], 32, LANES), F32),
            pltpu.VMEM((2, win_rows // 2, 2 * LANES), F32),
            pltpu.VMEM((2, win_rows // 2 + 16, win_cols), F32),
            pltpu.VMEM((sky, span + 2 * TILE_R, win_cols), BF16),
            pltpu.VMEM((sky, span + 2 * TILE_R, win_cols), BF16),
            pltpu.SemaphoreType.DMA((9,)),
            pltpu.SemaphoreType.DMA,
            pltpu.SemaphoreType.DMA,
        ],
        compiler_params=pltpu.CompilerParams(collective_id=0, has_side_effects=True),
        name="coadd",
    )(*inputs)
    coadd, weight_map = pl.pallas_call(
        hand_over,
        out_shape=(
            jax.ShapeDtypeStruct((owned_rows, win_cols), F32),
            jax.ShapeDtypeStruct((1, owned_rows), F32),
        ),
        in_specs=[vmem],
        out_specs=(vmem, vmem),
        name="hand_over",
    )(pltpu.with_memory_space_constraint(result, pltpu.VMEM))
    return coadd, weight_map.reshape(owned_rows)


def solution(mesh):
    return jax.shard_map(
        on_device,
        mesh=mesh,
        in_specs=(
            P(("groups", "sky"), None, None),
            P(),
            P(),
            P(("groups", "sky"), None, None),
            P(("groups", "sky"), None),
            P(("groups", "sky")),
            P("groups"),
            P(("groups", "sky")),
            P(("groups", "sky")),
        ),
        out_specs=(P(("groups", "sky"), None), P(("groups", "sky"))),
        check_vma=False,
    )
```
